128 devices in a mesh: trk: 16 (over z, y), mod: 8 (over x, core).
Axes of the slice: x: 4, y: 4, z: 4, core: 2. Of those that a mesh axis runs over, the one named last changes fastest.
Arguments:
- local_deriv: float32 [5, 12, 65536], P(None, None, ('trk', 'mod')), may hold values from -6 to 6
- global_deriv: float32 [8, 12, 65536], P(None, None, ('trk', 'mod')), may hold values from -6 to 6
- measured: float32 [12, 65536], P(None, ('trk', 'mod')), may hold values from -5 to 5
- hit_weight: float32 [12, 65536], P(None, ('trk', 'mod')), may hold values from 0.25 to 4
- hit_module: int32 [12, 65536], P(None, ('trk', 'mod')), may hold values from 0 to 65535, as said below
- hit_count: int32 [65536], P(('trk', 'mod')), may hold values from 6 to 12
- track_road: int32 [65536], P(('trk', 'mod')), may hold values from 0 to 8191, as said below
- road_start: int32 [8192], P(('trk', 'mod')), may hold values from 0 to 65535, as said below
- prior_weight: float32 [65536, 8], P(('trk', 'mod')), may hold values from 0.5 to 8
Outputs:
- normal_blocks: float32 [8192, 128, 128], P(('trk', 'mod'))
- rhs: float32 [65536, 8], P(('trk', 'mod'))
- corrections: float32 [65536, 8], P(('trk', 'mod'))
The draws below stay inside these ranges and needn't reach their ends.
Inputs may be any that keep to these rules, and one draw needn't show every extreme that they name: `hit_module`: each hit slot of track t, padding too, names one of the 16 modules (road_start[track_road[t]] + k) mod 65536, k = 0 to 15; the slots of one track name different modules. `track_road`: call the device that holds road_start[r] the owner of road r. At most 16 of the 512 tracks of one device belong to roads of one owner; one owner receives exactly 16 tracks from every device. road_start[r] lies between 16 / 2 * r and 16 / 2 * r + 16 / 2 - 1.
All inputs are finite; a program needn't handle non-finite values.
Results may differ from the reference program's by a relative error of at most 0.00016.
Values sent between devices are 32-bit elements; how exact they have to be, the bound alone decides.
A program may use at most 128 MiB of HBM per device.

```python
import math
import jax
import jax.numpy as jnp
from jax import lax

NPAR = 8
NLOC = 5
NHIT = 12
ROAD = 16
NMOD = 65536
TRK_DEV = 512
CAP = 16
TRACKS = 65536
NROAD = 8192
DEVICES = 128


def road_layout(key):
    spacing = ROAD // 2
    offsets = jax.random.randint(jax.random.fold_in(key, 11), (NROAD,), 0, spacing)
    road_index = jnp.arange(NROAD, dtype=jnp.int32)
    offsets = jnp.where(road_index == 0, 0, offsets)
    offsets = jnp.where(road_index == NROAD - 1, spacing - 1, offsets)
    return (spacing * road_index + offsets).astype(jnp.int32)


def track_owners(key):
    slot_total = DEVICES * CAP
    hot_rank = jax.random.permutation(jax.random.fold_in(key, 21), DEVICES)
    is_hot = hot_rank < DEVICES // 4
    slot_owner = jnp.arange(slot_total, dtype=jnp.int32) // CAP
    slot_rank = jnp.arange(slot_total, dtype=jnp.int32) % CAP
    available = jnp.where(is_hot[slot_owner], CAP, CAP // 4)
    unavailable = (slot_rank >= available).astype(jnp.int32)
    forced = (hot_rank[slot_owner] == 0).astype(jnp.int32)

    def shuffle_slots(one_key):
        return jax.random.permutation(one_key, slot_total)

    def shuffle_tracks(one_key):
        return jax.random.permutation(one_key, TRK_DEV)
    shuffled = jax.vmap(shuffle_slots)(jax.random.split(jax.random.fold_in(key, 23), DEVICES))
    scores = shuffled + slot_total * (1 + unavailable - forced)[None, :]
    chosen = jnp.argsort(scores, axis=1, stable=True)[:, :TRK_DEV]
    track_order = jax.vmap(shuffle_tracks)(jax.random.split(jax.random.fold_in(key, 24), DEVICES))
    chosen = jnp.take_along_axis(chosen, track_order, axis=1)
    owner_dev = chosen // CAP
    road_dev = NROAD // DEVICES
    local_road = jax.random.randint(jax.random.fold_in(key, 25), (DEVICES, TRK_DEV), 0, road_dev)
    return (owner_dev * road_dev + local_road).reshape(-1).astype(jnp.int32)


def hit_layout(key):
    starts = road_layout(key)
    road_ids = track_owners(key)
    scores = jax.random.randint(jax.random.fold_in(key, 31), (TRACKS, ROAD), 0, 1073741824)
    picked = jnp.argsort(scores, axis=1, stable=True)[:, :NHIT].astype(jnp.int32)
    modules = (starts[road_ids][:, None] + picked) % NMOD
    return (road_ids, modules.T.astype(jnp.int32))


def draw_road_start(key, part):
    return road_layout(key)


def draw_track_road(key, part):
    return hit_layout(key)[0]


def draw_hit_module(key, part):
    return hit_layout(key)[1]


def draw_measured(key, part):
    road_ids = track_owners(key)
    road_scale = 0.5 + road_ids.astype(jnp.float32) / NROAD
    values = jax.random.normal(jax.random.fold_in(key, 43), (NHIT, TRACKS), jnp.float32) * road_scale[None, :]
    return jnp.clip(values, -5.0, 5.0).astype(jnp.float32)


def plant(drawn, rng, smallest, largest):
    longest = drawn.shape.index(max(drawn.shape))
    spots = []
    for shift in (0, 1):
        where = [jax.random.randint(jax.random.fold_in(rng, axis), (), 0, length) for axis, length in enumerate(drawn.shape)]
        where[longest] = (where[longest] + shift) % drawn.shape[longest]
        spots.append(tuple(where))
    return drawn.at[spots[0]].set(smallest).at[spots[1]].set(largest)


def shard_levels(own_key, dims, shards, smallest, largest):
    def one(axis_at, parts):
        steps = jax.random.uniform(jax.random.fold_in(jax.random.fold_in(own_key, 6), axis_at), (parts,), jnp.float32, smallest / len(shards), largest / len(shards))
        return jnp.repeat(jnp.exp(steps), dims[axis_at] // parts).reshape((-1,) + (1,) * (len(dims) - axis_at - 1))

    gain = one(*shards[0])
    for cut in shards[1:]:
        gain = gain * one(*cut)
    return gain


def noise(key, shape, scale, most, cuts=(), kind=jnp.bfloat16):
    level = shard_levels(key, shape, cuts, -0.22, 0.18) if cuts else 1.0
    values = jax.random.normal(key, shape, jnp.float32) * scale * level
    return jnp.minimum(jnp.maximum(values, -most), most).astype(kind)


def setup_inputs(seed: int = 0) -> dict:
    seeds = jax.random.split(jax.random.key(seed), 10)
    local_deriv = noise(seeds[0], (NLOC, NHIT, TRACKS), 1.0, 6.0, ((2, 128),), jnp.float32)
    global_deriv = noise(seeds[1], (NPAR, NHIT, TRACKS), 1.0, 6.0, ((2, 128),), jnp.float32)
    measured = draw_measured(jax.random.fold_in(seeds[9], 71), 0)
    hit_weight = jnp.clip(jnp.exp(math.log(4.0) - 2.7725887 * jax.random.uniform(seeds[3], (NHIT, TRACKS), jnp.float32) ** shard_levels(seeds[3], (NHIT, TRACKS), ((1, 128),), -0.2, 0.2)), 0.25, 4.0)
    hit_module = draw_hit_module(jax.random.fold_in(seeds[9], 71), 0)
    hit_count = plant(jax.random.randint(seeds[5], (TRACKS,), 6, NHIT + 1), jax.random.fold_in(seeds[5], 1), 6, NHIT).astype(jnp.int32)
    track_road = draw_track_road(jax.random.fold_in(seeds[9], 71), 0)
    road_start = draw_road_start(jax.random.fold_in(seeds[9], 71), 0)
    prior_weight = jnp.clip(jnp.exp(math.log(8.0) - 2.7725887 * jax.random.uniform(seeds[8], (NMOD, NPAR), jnp.float32) ** shard_levels(seeds[8], (NMOD, NPAR), ((0, 128),), -0.2, 0.2)), 0.5, 8.0)
    return {"local_deriv": local_deriv, "global_deriv": global_deriv, "measured": measured, "hit_weight": hit_weight, "hit_module": hit_module, "hit_count": hit_count, "track_road": track_road, "road_start": road_start, "prior_weight": prior_weight}


EPS = 1e-06
HIGHEST = lax.Precision.HIGHEST

def local_fit(local_deriv, measured, hit_weight, hit_count):
    nlocal = local_deriv.shape[0]
    hit_slots = local_deriv.shape[1]
    position = lax.broadcasted_iota(jnp.int32, hit_weight.shape, 0)
    weight = jnp.where(position < hit_count[None, :], hit_weight, jnp.zeros_like(hit_weight))
    weighted = local_deriv * weight[None]
    local_gram = lax.optimization_barrier(jnp.sum(weighted[:, None] * local_deriv[None, :], axis=2))
    factor = {}
    for row_num in range(nlocal):
        for col_num in range(row_num + 1):
            running = local_gram[row_num, col_num]
            if row_num == col_num:
                running = running + 1.0
            for inner_num in range(col_num):
                running = running - factor[row_num, inner_num] * factor[col_num, inner_num]
            if row_num == col_num:
                factor[row_num, col_num] = jnp.sqrt(running)
            else:
                factor[row_num, col_num] = running / factor[col_num, col_num]
    solved_rows = []
    for row_num in range(nlocal):
        running = weighted[row_num]
        for col_num in range(row_num):
            running = running - factor[row_num, col_num][None] * solved_rows[col_num]
        solved_rows.append(running / factor[row_num, row_num][None])
    projected = jnp.stack(solved_rows)
    diagonal = jnp.eye(hit_slots, dtype=jnp.float32)[:, :, None] * weight[None]
    schur_block = diagonal - lax.optimization_barrier(jnp.sum(projected[:, :, None] * projected[:, None, :], axis=0))
    solved = lax.optimization_barrier(jnp.sum(schur_block * measured[None], axis=1))
    return (schur_block, solved)

def pair_blocks(global_rows, schur_rows):
    scaled_pairs = schur_rows[:, :, :, None] * global_rows[:, None, :, :]
    return global_rows[:, :, None, :, None] * scaled_pairs[:, :, :, None, :]

def minres_finish(beta_one, alpha_one, beta_two, alpha_two, beta_three, lanczos_one, lanczos_two):
    entry_first = alpha_one * alpha_one + beta_two * beta_two
    entry_cross = beta_two * (alpha_one + alpha_two)
    entry_second = beta_two * beta_two + alpha_two * alpha_two + beta_three * beta_three
    determinant = entry_first * entry_second - entry_cross * entry_cross
    coef_one = beta_one * (entry_second * alpha_one - entry_cross * beta_two) / determinant
    coef_two = beta_one * (entry_first * beta_two - entry_cross * alpha_one) / determinant
    return coef_one * lanczos_one + coef_two * lanczos_two

def apply_normal(vector, normal_blocks, gather_index, prior_weight):
    pieces = vector[gather_index].reshape(gather_index.shape[0], -1)
    mapped = jnp.einsum('rab,rb->ra', normal_blocks, pieces, precision=HIGHEST)
    spread = jnp.zeros_like(vector).at[gather_index.reshape(-1)].add(mapped.reshape(-1, vector.shape[1]))
    return prior_weight * vector + spread

def reference(local_deriv, global_deriv, measured, hit_weight, hit_module, hit_count, track_road, road_start, prior_weight):
    schur_block, solved = local_fit(local_deriv, measured, hit_weight, hit_count)
    slot_num = (hit_module - road_start[track_road][None, :]) % NMOD
    global_rows = jnp.transpose(global_deriv, (2, 1, 0))
    schur_rows = jnp.transpose(schur_block, (2, 0, 1))
    slot_rows = slot_num.T
    pair_index = track_road[:, None, None] * (ROAD * ROAD) + slot_rows[:, :, None] * ROAD + slot_rows[:, None, :]
    block_count = 16
    rows_each = TRACKS // block_count

    def accumulate(blocks, pieces):
        part_global, part_schur, part_index = pieces
        contrib = pair_blocks(part_global, part_schur).reshape(-1, NPAR, NPAR)
        return (blocks.at[part_index.reshape(-1)].add(contrib), None)
    start_blocks = jnp.zeros((NROAD * ROAD * ROAD, NPAR, NPAR), jnp.float32)
    blocks, unused = lax.scan(accumulate, start_blocks, (global_rows.reshape(block_count, rows_each, NHIT, NPAR), schur_rows.reshape(block_count, rows_each, NHIT, NHIT), pair_index.reshape(block_count, rows_each, NHIT, NHIT)))
    normal_blocks = blocks.reshape(NROAD, ROAD, ROAD, NPAR, NPAR).transpose(0, 1, 3, 2, 4).reshape(NROAD, ROAD * NPAR, ROAD * NPAR)
    rhs = jnp.zeros((NMOD, NPAR), jnp.float32).at[hit_module.T.reshape(-1)].add((global_rows * solved.T[:, :, None]).reshape(-1, NPAR))
    gather_index = (road_start[:, None] + jnp.arange(ROAD, dtype=jnp.int32)[None, :]) % NMOD

    def apply_here(vector):
        return apply_normal(vector, normal_blocks, gather_index, prior_weight)
    beta_one = jnp.sqrt(jnp.sum(rhs * rhs) + EPS)
    lanczos_one = rhs / beta_one
    mapped = apply_here(lanczos_one)
    alpha_one = jnp.sum(lanczos_one * mapped)
    residue = mapped - alpha_one * lanczos_one
    beta_two = jnp.sqrt(jnp.sum(residue * residue) + EPS)
    lanczos_two = residue / beta_two
    mapped = apply_here(lanczos_two) - beta_two * lanczos_one
    alpha_two = jnp.sum(lanczos_two * mapped)
    residue = mapped - alpha_two * lanczos_two
    beta_three = jnp.sqrt(jnp.sum(residue * residue) + EPS)
    corrections = minres_finish(beta_one, alpha_one, beta_two, alpha_two, beta_three, lanczos_one, lanczos_two)
    return (normal_blocks, rhs, corrections)
```

```python
import functools

import jax
import jax.numpy as jnp
from jax import lax
from jax.experimental import pallas as pl
from jax.experimental.pallas import tpu as pltpu
from jax.sharding import PartitionSpec as P

F32 = jnp.float32
BF16 = jnp.bfloat16
NPAR = 8
NLOC = 5
NHIT = 12
ROAD = 16
CAP = 16
LANE = 128
NMOD = 65536
ROADS = 64
TRACKS = 512
DEV = 128
GROUP = 16
EPS = 1e-6
MESH = pl.DeviceIdType.MESH
CONTRACT_LANES = (((1,), (1,)), ((), ()))


def dot_t(a, b):
    return lax.dot_general(a, b, CONTRACT_LANES, preferred_element_type=F32)


def split(x):
    hi = x.astype(BF16)
    return hi, (x - hi.astype(F32)).astype(BF16)


def fit_and_place(ld, gd, me, hw, hm, hc, tr, send, lay):
    position = lax.broadcasted_iota(jnp.int32, (NHIT, TRACKS), 0)
    live = position < hc[...]
    root = jnp.where(live, jnp.sqrt(hw[...]), 0.0)
    scaled = [ld[a] * root for a in range(NLOC)]
    factor = {}
    for i in range(NLOC):
        for j in range(i + 1):
            running = jnp.sum(scaled[i] * scaled[j], axis=0, keepdims=True)
            if i == j:
                running = running + 1.0
            for k in range(j):
                running = running - factor[i, k] * factor[j, k]
            factor[i, j] = jnp.sqrt(running) if i == j else running / factor[j, j]
    proj = []
    for i in range(NLOC):
        running = scaled[i]
        for j in range(i):
            running = running - factor[i, j] * proj[j]
        proj.append(running / factor[i, i])
    resid = me[...] * root
    solved = resid
    for a in range(NLOC):
        solved = solved - proj[a] * jnp.sum(proj[a] * resid, axis=0, keepdims=True)
    road = tr[...]
    rel = lax.rem(hm[...] - NPAR * road + NMOD, NMOD).astype(F32)
    local_road = jnp.broadcast_to((road & (ROADS - 1)).astype(F32), (NHIT, TRACKS))
    words = [gd[p] * root for p in range(NPAR)] + proj + [solved, rel, local_road]
    for w, value in enumerate(words):
        for c in range(TRACKS // LANE):
            part = value[:, c * LANE : (c + 1) * LANE]
            lay[c, pl.ds(w, 8, stride=16), :] = part[:8]
            lay[c, pl.ds(LANE + w, 4, stride=16), :] = part[8:]
    whole = jnp.concatenate([lay[c] for c in range(TRACKS // LANE)], axis=1)
    first_hi, first_lo = split(whole[:LANE])
    tail = whole[LANE:]
    none = jnp.zeros_like(tail)
    left_hi, left_lo = split(jnp.concatenate([tail, none], axis=0))
    right_hi, right_lo = split(jnp.concatenate([none, tail], axis=0))

    owner = road >> 6
    mine = lax.broadcasted_iota(jnp.int32, (DEV, TRACKS), 0) == owner
    member = jnp.where(mine, 1.0, 0.0)
    earlier = lax.broadcasted_iota(jnp.int32, (TRACKS, TRACKS), 0) <= lax.broadcasted_iota(
        jnp.int32, (TRACKS, TRACKS), 1
    )
    running = jnp.dot(
        member.astype(BF16), jnp.where(earlier, 1.0, 0.0).astype(BF16), preferred_element_type=F32
    )
    rank = jnp.sum(member * running, axis=0, keepdims=True) - 1.0
    slot = owner * CAP + rank.astype(jnp.int32)

    def place(step, carry):
        row = lax.broadcasted_iota(jnp.int32, (GROUP * CAP, TRACKS), 0) + step * (GROUP * CAP)
        chosen = jnp.where(row == slot, 1.0, 0.0)
        pick = chosen.astype(BF16)
        first = dot_t(pick, first_hi) + dot_t(pick, first_lo)
        halves = chosen.reshape(GROUP, 2, 8, TRACKS)
        low = halves[:, 0].reshape(LANE, TRACKS).astype(BF16)
        high = halves[:, 1].reshape(LANE, TRACKS).astype(BF16)
        last = dot_t(low, left_hi) + dot_t(low, left_lo) + dot_t(high, right_hi) + dot_t(high, right_lo)
        at = pl.ds(pl.multiple_of(step * GROUP, GROUP), GROUP)
        send[at, 0:16, :] = first.reshape(GROUP, CAP, LANE)
        send[at, 16:24, :] = last.reshape(GROUP, 8, LANE)
        return carry

    lax.fori_loop(0, DEV // GROUP, place, 0)


def kernel_send(ld, gd, me, hw, hm, hc, tr, send, lay):
    fit_and_place(ld, gd, me, hw, hm, hc, tr, send, lay)


def assemble(x, off, blocks, road_rhs, g_ref, x_ref, hot_ref, mix_ref, z_ref):
    t0 = x[:, 0:8, :].reshape(LANE, LANE).T
    t1 = x[:, 8:16, :].reshape(LANE, LANE).T
    t2 = x[:, 16:24, :].reshape(LANE, LANE).T
    body = jnp.concatenate([t0, t1], axis=1)
    tail = jnp.concatenate([t2[:64], t2[64:]], axis=1)
    hits = []
    for i in range(NHIT):
        source, row = (body, 16 * i) if i < 8 else (tail, 16 * (i - 8))
        hits.append((source[row : row + 8], source[row + 8 : row + 16]))
    wide = 2 * LANE
    road = hits[0][1][7:8]
    each = lax.broadcasted_iota(jnp.int32, (ROADS, wide), 0).astype(F32)
    hot = jnp.where(each == road, 1.0, 0.0)
    start = jnp.sum(hot * off, axis=0, keepdims=True)
    rows = (lax.broadcasted_iota(jnp.int32, (ROADS * NPAR, wide), 0) >> 3).astype(F32)
    hot_ref[...] = jnp.where(rows == road, 1.0, 0.0).astype(BF16)
    slots = [jnp.broadcast_to(hits[i][1][6:7] - start, (8, wide)) for i in range(NHIT)]
    sums = []
    for s in range(ROAD):
        g = jnp.zeros((8, wide), F32)
        a = jnp.zeros((8, wide), F32)
        for i in range(NHIT):
            same = slots[i] == float(s)
            g = jnp.where(same, hits[i][0], g)
            a = jnp.where(same, hits[i][1], a)
        g_ref[8 * s : 8 * s + 8, :] = g
        x_ref[0, 8 * s : 8 * s + 8, :] = a[:, :LANE]
        x_ref[1, 8 * s : 8 * s + 8, :] = a[:, LANE:]
        sums.append(g * a[5:6])
    v_hi, v_lo = split(jnp.concatenate(sums, axis=0))
    hot16 = hot.astype(BF16)
    road_rhs[...] += dot_t(hot16, v_hi) + dot_t(hot16, v_lo)
    lines = [
        jnp.concatenate(
            [x_ref[c, pl.ds(a, ROAD, stride=8), :] for c in range(2)], axis=1
        )
        for a in range(NLOC)
    ]

    def slot_step(s, carry):
        at = pl.ds(pl.multiple_of(s * 8, 8), 8)
        g_s = g_ref[at, :]
        a_s = jnp.concatenate([x_ref[0, at, :], x_ref[1, at, :]], axis=1)
        mix = jnp.where(lax.broadcasted_iota(jnp.int32, (ROAD, wide), 0) == s, 1.0, 0.0)
        for a in range(NLOC):
            mix = mix - a_s[a : a + 1] * lines[a]
        mix_ref[...] = mix
        for u in range(ROAD):
            z = g_ref[8 * u : 8 * u + 8, :] * mix_ref[u : u + 1, :]
            z_ref[8 * u : 8 * u + 8, :] = z
        z_hi, z_lo = split(z_ref[...])
        pair = jnp.concatenate([g_s, g_s], axis=0)
        g_hi, g_lo = split(pair)
        hot = hot_ref[...].reshape(ROADS // 2, 16, wide)
        left_hi = (hot * g_hi[None]).reshape(ROADS * NPAR, wide)
        left_lo = (hot * g_lo[None]).reshape(ROADS * NPAR, wide)
        out = dot_t(left_hi, z_hi) + dot_t(left_hi, z_lo) + dot_t(left_lo, z_hi)
        blocks[:, at, :] += out.reshape(ROADS, NPAR, LANE)
        return carry

    lax.fori_loop(0, ROAD, slot_step, 0)


def kernel_assemble(x, off, blocks, road_rhs, g_ref, x_ref, hot_ref, mix_ref, z_ref):
    @pl.when(pl.program_id(0) == 0)
    def _():
        blocks[...] = jnp.zeros_like(blocks)
        road_rhs[...] = jnp.zeros_like(road_rhs)

    assemble(x[...], off[...], blocks, road_rhs, g_ref, x_ref, hot_ref, mix_ref, z_ref)


HALF = 64


def low_lanes(x):
    return jnp.where(lax.broadcasted_iota(jnp.int32, x.shape, 1) < HALF, x, 0.0)


def spread(pieces, off, field):
    wide = jnp.concatenate([pieces, jnp.zeros_like(pieces)], axis=1)
    moved = jnp.where(off == 0.0, wide, 0.0)
    for d in range(1, NPAR):
        moved = jnp.where(off == float(d), pltpu.roll(wide, 8 * d, 1), moved)
    head, rest = moved[:, :LANE], moved[:, LANE:]
    field[...] = jnp.zeros_like(field)
    field[0:64, :] = low_lanes(head)
    field[1:65, :] += low_lanes(pltpu.roll(head, HALF, 1))
    field[2:66, :] += low_lanes(rest)


def gather(field, off):
    head = field[0:64, :] + pltpu.roll(field[1:65, :], HALF, 1)
    wide = jnp.concatenate([head, field[2:66, :]], axis=1)
    piece = jnp.where(off == 0.0, wide, 0.0)
    for d in range(1, NPAR):
        piece = jnp.where(off == float(d), pltpu.roll(wide, 2 * LANE - 8 * d, 1), piece)
    return piece[:, :LANE]


def total(x):
    return jnp.sum(jnp.sum(x, axis=0, keepdims=True), axis=1, keepdims=True)


def krylov(blocks, road_rhs, off, prior, rhs_out, cor_out, field, vec, image, mapped, up, down,
           from_prev, from_next, line, lines, sems, gsem):
    trk, mod = lax.axis_index("trk"), lax.axis_index("mod")
    me = trk * 8 + mod
    nxt = lax.rem(me + 1, DEV)
    prv = lax.rem(me + DEV - 1, DEV)
    off = off[...]

    def place(d):
        return (d // 8, lax.rem(d, 8))

    def exchange(e, target):
        up[e] = field[64:72, :]
        down[e] = field[0:8, :]
        to_next = pltpu.make_async_remote_copy(
            up.at[e], from_prev.at[e], sems.at[e, 0], sems.at[e, 1], device_id=place(nxt), device_id_type=MESH
        )
        to_prev = pltpu.make_async_remote_copy(
            down.at[e], from_next.at[e], sems.at[e, 2], sems.at[e, 3], device_id=place(prv), device_id_type=MESH
        )
        to_next.start()
        to_prev.start()
        target[8:64, :] = field[8:64, :]
        to_next.wait()
        to_prev.wait()
        keep = lax.broadcasted_iota(jnp.int32, (8, LANE), 0) < 2
        target[0:8, :] = field[0:8, :] + jnp.where(keep, from_prev[e], 0.0)
        target[64:72, :] = jnp.where(keep, field[64:72, :] + from_next[e], 0.0)

    def apply(source, e, target):
        piece = gather(source, off)
        flipped = piece.T
        for r in range(ROADS):
            row = jnp.sum(blocks[r] * flipped[:, r : r + 1], axis=0, keepdims=True)
            mapped[r : r + 1, :] = row
        spread(mapped[...], off, field)
        field[0:64, :] += prior[...] * source[0:64, :]
        exchange(e, target)

    spread(road_rhs[...], off, field)
    exchange(0, vec.at[0])
    rhs_out[...] = vec[0, 0:64, :]
    apply(vec.at[0], 1, vec.at[1])
    apply(vec.at[1], 2, vec.at[2])
    b, w, u = vec[0, 0:64, :], vec[1, 0:64, :], vec[2, 0:64, :]

    def unit(norm):
        return jnp.where(norm > 0.0, 1.0 / jnp.where(norm > 0.0, norm, 1.0), 0.0)

    r11 = jnp.sqrt(total(b * b))
    q1 = b * unit(r11)
    r12 = total(q1 * w)
    r13 = total(q1 * u)
    w1 = w - r12 * q1
    u1 = u - r13 * q1
    r22 = jnp.sqrt(total(w1 * w1))
    q2 = w1 * unit(r22)
    r23 = total(q2 * u1)
    u2 = u1 - r23 * q2
    r33 = jnp.sqrt(total(u2 * u2))
    lane = lax.broadcasted_iota(jnp.int32, (1, LANE), 1)
    row = jnp.zeros((1, LANE), F32)
    for n, value in enumerate((r11, r12, r13, r22, r23, r33)):
        row = jnp.where(lane == n, value, row)
    line[...] = row
    lines[me] = row

    def send_line(k, carry):
        other = lax.rem(me + k, DEV)
        pltpu.make_async_remote_copy(
            line, lines.at[me], gsem.at[0], gsem.at[1], device_id=place(other), device_id_type=MESH
        ).start()
        return carry

    lax.fori_loop(1, DEV, send_line, 0)
    whole = pltpu.make_async_remote_copy(
        lines.at[pl.ds(0, DEV - 1)], lines.at[pl.ds(0, DEV - 1)], gsem.at[0], gsem.at[1],
        device_id=place(nxt), device_id_type=MESH,
    )
    whole.wait_recv()
    every = lines[...]

    def col(n):
        return every[:, :, n : n + 1]

    def add(x):
        return jnp.sum(x, axis=0)

    b0, w0, u0, w1, u1, u2 = (col(n) for n in range(6))
    beta_one = jnp.sqrt(add(b0 * b0) + EPS)
    inv_one = 1.0 / beta_one
    b0 = b0 * inv_one
    w0, w1 = w0 * inv_one, w1 * inv_one
    u0, u1, u2 = u0 * inv_one, u1 * inv_one, u2 * inv_one
    alpha_one = add(b0 * w0)
    x0, x1 = w0 - alpha_one * b0, w1
    beta_two = jnp.sqrt(add(x0 * x0 + x1 * x1) + EPS)
    inv_two = 1.0 / beta_two
    x0, x1 = x0 * inv_two, x1 * inv_two
    y0 = (u0 - alpha_one * w0) * inv_two - beta_two * b0
    y1 = (u1 - alpha_one * w1) * inv_two
    y2 = u2 * inv_two
    alpha_two = add(x0 * y0 + x1 * y1)
    y0, y1 = y0 - alpha_two * x0, y1 - alpha_two * x1
    beta_three = jnp.sqrt(add(y0 * y0 + y1 * y1 + y2 * y2) + EPS)
    first = alpha_one * alpha_one + beta_two * beta_two
    cross = beta_two * (alpha_one + alpha_two)
    second = beta_two * beta_two + alpha_two * alpha_two + beta_three * beta_three
    determinant = first * second - cross * cross
    coef_one = beta_one * (second * alpha_one - cross * beta_two) / determinant
    coef_two = beta_one * (first * beta_two - cross * alpha_one) / determinant
    v1 = b * inv_one
    v2 = (w * inv_one - alpha_one * v1) * inv_two
    cor_out[...] = coef_one * v1 + coef_two * v2
    whole.wait_send()


def kernel_krylov(*refs):
    trk, mod = lax.axis_index("trk"), lax.axis_index("mod")
    me = trk * 8 + mod
    barrier = pltpu.get_barrier_semaphore()

    def greet(k, carry):
        other = lax.rem(me + k, DEV)
        pl.semaphore_signal(
            barrier, inc=1, device_id=(other // 8, lax.rem(other, 8)), device_id_type=MESH
        )
        return carry

    lax.fori_loop(1, DEV, greet, 0)
    pl.semaphore_wait(barrier, DEV - 1)
    krylov(*refs)


VM = pl.BlockSpec(memory_space=pltpu.VMEM)


def on_device(ld, gd, me, hw, hm, hc, tr, rs, pw):
    send = pl.pallas_call(
        kernel_send,
        out_shape=jax.ShapeDtypeStruct((DEV, 24, LANE), F32),
        in_specs=[VM] * 7,
        out_specs=VM,
        scratch_shapes=[pltpu.VMEM((4, 192, LANE), F32)],
        name="fit_place",
    )(ld, gd, me, hw, hm, hc.reshape(1, TRACKS), tr.reshape(1, TRACKS))
    recv = lax.all_to_all(send, ("trk", "mod"), split_axis=0, concat_axis=0, tiled=True)
    off = (rs % NPAR).astype(F32).reshape(ROADS, 1)
    blocks, road_rhs = pl.pallas_call(
        kernel_assemble,
        grid=(DEV // GROUP,),
        out_shape=(
            jax.ShapeDtypeStruct((ROADS, LANE, LANE), F32),
            jax.ShapeDtypeStruct((ROADS, LANE), F32),
        ),
        in_specs=[
            pl.BlockSpec((GROUP, 24, LANE), lambda c: (c, 0, 0)),
            pl.BlockSpec((ROADS, 1), lambda c: (0, 0)),
        ],
        out_specs=(
            pl.BlockSpec((ROADS, LANE, LANE), lambda c: (0, 0, 0)),
            pl.BlockSpec((ROADS, LANE), lambda c: (0, 0)),
        ),
        scratch_shapes=[
            pltpu.VMEM((LANE, 2 * LANE), F32),
            pltpu.VMEM((2, LANE, LANE), F32),
            pltpu.VMEM((ROADS * NPAR, 2 * LANE), BF16),
            pltpu.VMEM((ROAD, 2 * LANE), F32),
            pltpu.VMEM((LANE, 2 * LANE), F32),
        ],
        name="assemble",
    )(recv, off)
    prior = jnp.pad(pw.reshape(HALF, HALF), ((0, 0), (0, HALF)))
    rhs, cor = pl.pallas_call(
        kernel_krylov,
        out_shape=(jax.ShapeDtypeStruct((HALF, LANE), F32), jax.ShapeDtypeStruct((HALF, LANE), F32)),
        in_specs=[VM] * 4,
        out_specs=(VM, VM),
        scratch_shapes=[
            pltpu.VMEM((72, LANE), F32),
            pltpu.VMEM((3, 72, LANE), F32),
            pltpu.VMEM((72, LANE), F32),
            pltpu.VMEM((ROADS, LANE), F32),
            pltpu.VMEM((3, 8, LANE), F32),
            pltpu.VMEM((3, 8, LANE), F32),
            pltpu.VMEM((3, 8, LANE), F32),
            pltpu.VMEM((3, 8, LANE), F32),
            pltpu.VMEM((1, LANE), F32),
            pltpu.VMEM((DEV, 1, LANE), F32),
            pltpu.SemaphoreType.DMA((3, 4)),
            pltpu.SemaphoreType.DMA((2,)),
        ],
        compiler_params=pltpu.CompilerParams(collective_id=0, has_side_effects=True),
        name="krylov",
    )(blocks, road_rhs, off, prior)
    return (
        blocks,
        rhs[:, :HALF].reshape(TRACKS, NPAR),
        cor[:, :HALF].reshape(TRACKS, NPAR),
    )


def solution(mesh):
    both = ("trk", "mod")
    in_specs = (
        P(None, None, both),
        P(None, None, both),
        P(None, both),
        P(None, both),
        P(None, both),
        P(both),
        P(both),
        P(both),
        P(both, None),
    )
    out_specs = (P(both, None, None), P(both, None), P(both, None))
    return jax.shard_map(on_device, mesh=mesh, in_specs=in_specs, out_specs=out_specs, check_vma=False)
```

```python
import functools

import jax
import jax.numpy as jnp
from jax import lax
from jax.experimental import pallas as pl
from jax.experimental.pallas import tpu as pltpu
from jax.sharding import PartitionSpec as P

F32 = jnp.float32
BF16 = jnp.bfloat16
NPAR = 8
NLOC = 5
NHIT = 12
ROAD = 16
CAP = 16
LANE = 128
NMOD = 65536
ROADS = 64
TRACKS = 512
DEV = 128
GROUP = 16
PLACED = 32
EPS = 1e-6
MESH = pl.DeviceIdType.MESH
CONTRACT_LANES = (((1,), (1,)), ((), ()))


def dot_t(a, b):
    return lax.dot_general(a, b, CONTRACT_LANES, preferred_element_type=F32)


def split(x):
    hi = x.astype(BF16)
    return hi, (x - hi.astype(F32)).astype(BF16)


def fit_and_place(ld, gd, me, hw, hm, hc, tr, send, lay):
    position = lax.broadcasted_iota(jnp.int32, (NHIT, TRACKS), 0)
    live = position < hc[...]
    root = jnp.where(live, jnp.sqrt(hw[...]), 0.0)
    scaled = [ld[a] * root for a in range(NLOC)]
    factor = {}
    for i in range(NLOC):
        for j in range(i + 1):
            running = jnp.sum(scaled[i] * scaled[j], axis=0, keepdims=True)
            if i == j:
                running = running + 1.0
            for k in range(j):
                running = running - factor[i, k] * factor[j, k]
            factor[i, j] = jnp.sqrt(running) if i == j else running / factor[j, j]
    proj = []
    for i in range(NLOC):
        running = scaled[i]
        for j in range(i):
            running = running - factor[i, j] * proj[j]
        proj.append(running / factor[i, i])
    resid = me[...] * root
    solved = resid
    for a in range(NLOC):
        solved = solved - proj[a] * jnp.sum(proj[a] * resid, axis=0, keepdims=True)
    road = tr[...]
    rel = lax.rem(hm[...] - NPAR * road + NMOD, NMOD).astype(F32)
    local_road = jnp.broadcast_to((road & (ROADS - 1)).astype(F32), (NHIT, TRACKS))
    words = proj + [solved, rel, local_road]
    for c in range(TRACKS // LANE):
        at = slice(c * LANE, (c + 1) * LANE)
        for i in range(NHIT):
            lay[c, 16 * i : 16 * i + 8, :] = gd[i, :, at] * root[i : i + 1, at]
        for w, value in enumerate(words):
            lay[c, pl.ds(8 + w, 8, stride=16), :] = value[:8, at]
            lay[c, pl.ds(LANE + 8 + w, 4, stride=16), :] = value[8:, at]
    whole = jnp.concatenate([lay[c] for c in range(TRACKS // LANE)], axis=1)
    tail = whole[LANE:]
    none = jnp.zeros_like(tail)

    def both(value):
        return jnp.concatenate(split(value), axis=0)

    first_w = both(whole[:LANE])
    left_w = both(jnp.concatenate([tail, none], axis=0))
    right_w = both(jnp.concatenate([none, tail], axis=0))

    owner = road >> 6
    mine = lax.broadcasted_iota(jnp.int32, (DEV, TRACKS), 0) == owner
    member = jnp.where(mine, 1.0, 0.0)
    earlier = lax.broadcasted_iota(jnp.int32, (TRACKS, TRACKS), 0) <= lax.broadcasted_iota(
        jnp.int32, (TRACKS, TRACKS), 1
    )
    running = jnp.dot(
        member.astype(BF16), jnp.where(earlier, 1.0, 0.0).astype(BF16), preferred_element_type=F32
    )
    rank = jnp.sum(member * running, axis=0, keepdims=True) - 1.0
    slot = owner * CAP + rank.astype(jnp.int32)

    def place(step, carry):
        row = lax.broadcasted_iota(jnp.int32, (PLACED * CAP, TRACKS), 0) + step * (PLACED * CAP)
        chosen = jnp.where(row == slot, 1.0, 0.0)
        halves = chosen.reshape(PLACED, 2, 8, TRACKS)
        low = halves[:, 0].reshape(PLACED * 8, TRACKS).astype(BF16)
        high = halves[:, 1].reshape(PLACED * 8, TRACKS).astype(BF16)
        first = dot_t(chosen.astype(BF16), first_w)
        last = dot_t(low, left_w) + dot_t(high, right_w)
        at = pl.ds(pl.multiple_of(step * PLACED, PLACED), PLACED)
        send[at, 0:16, :] = (first[:, :LANE] + first[:, LANE:]).reshape(PLACED, CAP, LANE)
        send[at, 16:24, :] = (last[:, :LANE] + last[:, LANE:]).reshape(PLACED, 8, LANE)
        return carry

    lax.fori_loop(0, DEV // PLACED, place, 0)


def kernel_send(ld, gd, me, hw, hm, hc, tr, send, lay):
    fit_and_place(ld, gd, me, hw, hm, hc, tr, send, lay)


def assemble(x, off, blocks, road_rhs, g_ref, t_ref, x_ref, hot_ref, mix_ref, z_ref):
    t0 = x[:, 0:8, :].reshape(LANE, LANE).T
    t1 = x[:, 8:16, :].reshape(LANE, LANE).T
    t2 = x[:, 16:24, :].reshape(LANE, LANE).T
    body = jnp.concatenate([t0, t1], axis=1)
    tail = jnp.concatenate([t2[:64], t2[64:]], axis=1)
    hits = []
    for i in range(NHIT):
        source, row = (body, 16 * i) if i < 8 else (tail, 16 * (i - 8))
        hits.append((source[row : row + 8], source[row + 8 : row + 16]))
    wide = 2 * LANE
    road = hits[0][1][7:8]
    each = lax.broadcasted_iota(jnp.int32, (ROADS, wide), 0).astype(F32)
    hot = jnp.where(each == road, 1.0, 0.0)
    start = jnp.sum(hot * off, axis=0, keepdims=True)
    rows = (lax.broadcasted_iota(jnp.int32, (ROADS * NPAR, wide), 0) >> 3).astype(F32)
    hot_ref[...] = jnp.where(rows == road, 1.0, 0.0).astype(BF16)
    slots = [jnp.broadcast_to(hits[i][1][6:7] - start, (8, wide)) for i in range(NHIT)]
    sums = []
    for s in range(ROAD):
        g = jnp.zeros((8, wide), F32)
        a = jnp.zeros((8, wide), F32)
        for i in range(NHIT):
            same = slots[i] == float(s)
            g = jnp.where(same, hits[i][0], g)
            a = jnp.where(same, hits[i][1], a)
        g_ref[8 * s : 8 * s + 8, :] = g
        t_ref[8 * s : 8 * s + 8, :] = 2.0 * g - g.astype(BF16).astype(F32)
        x_ref[0, 8 * s : 8 * s + 8, :] = a[:, :LANE]
        x_ref[1, 8 * s : 8 * s + 8, :] = a[:, LANE:]
        sums.append(g * a[5:6])
    v_hi, v_lo = split(jnp.concatenate(sums, axis=0))
    hot16 = hot.astype(BF16)
    road_rhs[...] += dot_t(hot16, v_hi) + dot_t(hot16, v_lo)
    lines = [
        jnp.concatenate(
            [x_ref[c, pl.ds(a, ROAD, stride=8), :] for c in range(2)], axis=1
        )
        for a in range(NLOC)
    ]

    def slot_step(s, carry):
        at = pl.ds(pl.multiple_of(s * 8, 8), 8)
        g_s = g_ref[at, :]
        a_s = jnp.concatenate([x_ref[0, at, :], x_ref[1, at, :]], axis=1)
        mix = jnp.where(lax.broadcasted_iota(jnp.int32, (ROAD, wide), 0) == s, 1.0, 0.0)
        for a in range(NLOC):
            mix = mix - a_s[a : a + 1] * lines[a]
        mix_ref[...] = mix
        for u in range(ROAD):
            z = t_ref[8 * u : 8 * u + 8, :] * mix_ref[u : u + 1, :]
            z_ref[8 * u : 8 * u + 8, :] = z
        z_both = jnp.concatenate(split(z_ref[...]), axis=0)
        g_hi = jnp.concatenate([g_s, g_s], axis=0).astype(BF16)
        hot = hot_ref[...].reshape(ROADS // 2, 16, wide)
        left = (hot * g_hi[None]).reshape(ROADS * NPAR, wide)
        out = dot_t(left, z_both)
        blocks[:, at, :] += (out[:, :LANE] + out[:, LANE:]).reshape(ROADS, NPAR, LANE)
        return carry

    lax.fori_loop(0, ROAD, slot_step, 0, unroll=2)


def symmetric(blocks):
    def one(r, carry):
        block = blocks[r]
        blocks[r] = 0.5 * (block + block.T)
        return carry

    lax.fori_loop(0, ROADS, one, 0, unroll=4)


def kernel_assemble(x, off, blocks, road_rhs, g_ref, t_ref, x_ref, hot_ref, mix_ref, z_ref):
    @pl.when(pl.program_id(0) == 0)
    def _():
        blocks[...] = jnp.zeros_like(blocks)
        road_rhs[...] = jnp.zeros_like(road_rhs)

    assemble(x[...], off[...], blocks, road_rhs, g_ref, t_ref, x_ref, hot_ref, mix_ref, z_ref)

    @pl.when(pl.program_id(0) == pl.num_programs(0) - 1)
    def _():
        symmetric(blocks)


HALF = 64


def low_lanes(x):
    return jnp.where(lax.broadcasted_iota(jnp.int32, x.shape, 1) < HALF, x, 0.0)


def spread(pieces, off, field):
    wide = jnp.concatenate([pieces, jnp.zeros_like(pieces)], axis=1)
    moved = jnp.where(off == 0.0, wide, 0.0)
    for d in range(1, NPAR):
        moved = jnp.where(off == float(d), pltpu.roll(wide, 8 * d, 1), moved)
    head, rest = moved[:, :LANE], moved[:, LANE:]
    field[...] = jnp.zeros_like(field)
    field[0:64, :] = low_lanes(head)
    field[1:65, :] += low_lanes(pltpu.roll(head, HALF, 1))
    field[2:66, :] += low_lanes(rest)


def gather(field, off):
    head = field[0:64, :] + pltpu.roll(field[1:65, :], HALF, 1)
    wide = jnp.concatenate([head, field[2:66, :]], axis=1)
    piece = jnp.where(off == 0.0, wide, 0.0)
    for d in range(1, NPAR):
        piece = jnp.where(off == float(d), pltpu.roll(wide, 2 * LANE - 8 * d, 1), piece)
    return piece[:, :LANE]


def total(x):
    return jnp.sum(jnp.sum(x, axis=0, keepdims=True), axis=1, keepdims=True)


def krylov(blocks, road_rhs, off, prior, rhs_out, cor_out, field, vec, image, mapped, up, down,
           from_prev, from_next, line, lines, sems, gsem):
    trk, mod = lax.axis_index("trk"), lax.axis_index("mod")
    me = trk * 8 + mod
    nxt = lax.rem(me + 1, DEV)
    prv = lax.rem(me + DEV - 1, DEV)
    off = off[...]

    def place(d):
        return (d // 8, lax.rem(d, 8))

    def exchange(e, target):
        up[e] = field[64:72, :]
        down[e] = field[0:8, :]
        to_next = pltpu.make_async_remote_copy(
            up.at[e], from_prev.at[e], sems.at[e, 0], sems.at[e, 1], device_id=place(nxt), device_id_type=MESH
        )
        to_prev = pltpu.make_async_remote_copy(
            down.at[e], from_next.at[e], sems.at[e, 2], sems.at[e, 3], device_id=place(prv), device_id_type=MESH
        )
        to_next.start()
        to_prev.start()
        target[8:64, :] = field[8:64, :]
        to_next.wait()
        to_prev.wait()
        keep = lax.broadcasted_iota(jnp.int32, (8, LANE), 0) < 2
        target[0:8, :] = field[0:8, :] + jnp.where(keep, from_prev[e], 0.0)
        target[64:72, :] = jnp.where(keep, field[64:72, :] + from_next[e], 0.0)

    def apply(source, e, target):
        piece = gather(source, off)
        flipped = piece.T
        for r in range(ROADS):
            row = jnp.sum(blocks[r] * flipped[:, r : r + 1], axis=0, keepdims=True)
            mapped[r : r + 1, :] = row
        spread(mapped[...], off, field)
        field[0:64, :] += prior[...] * source[0:64, :]
        exchange(e, target)

    spread(road_rhs[...], off, field)
    exchange(0, vec.at[0])
    rhs_out[...] = vec[0, 0:64, :]
    apply(vec.at[0], 1, vec.at[1])
    apply(vec.at[1], 2, vec.at[2])
    b, w, u = vec[0, 0:64, :], vec[1, 0:64, :], vec[2, 0:64, :]

    def unit(norm):
        return jnp.where(norm > 0.0, 1.0 / jnp.where(norm > 0.0, norm, 1.0), 0.0)

    r11 = jnp.sqrt(total(b * b))
    q1 = b * unit(r11)
    r12 = total(q1 * w)
    r13 = total(q1 * u)
    w1 = w - r12 * q1
    u1 = u - r13 * q1
    r22 = jnp.sqrt(total(w1 * w1))
    q2 = w1 * unit(r22)
    r23 = total(q2 * u1)
    u2 = u1 - r23 * q2
    r33 = jnp.sqrt(total(u2 * u2))
    lane = lax.broadcasted_iota(jnp.int32, (1, LANE), 1)
    row = jnp.zeros((1, LANE), F32)
    for n, value in enumerate((r11, r12, r13, r22, r23, r33)):
        row = jnp.where(lane == n, value, row)
    line[...] = row
    lines[me] = row

    def send_line(k, carry):
        other = lax.rem(me + k, DEV)
        pltpu.make_async_remote_copy(
            line, lines.at[me], gsem.at[0], gsem.at[1], device_id=place(other), device_id_type=MESH
        ).start()
        return carry

    lax.fori_loop(1, DEV, send_line, 0)
    whole = pltpu.make_async_remote_copy(
        lines.at[pl.ds(0, DEV - 1)], lines.at[pl.ds(0, DEV - 1)], gsem.at[0], gsem.at[1],
        device_id=place(nxt), device_id_type=MESH,
    )
    whole.wait_recv()
    every = lines[...]

    def col(n):
        return every[:, :, n : n + 1]

    def add(x):
        return jnp.sum(x, axis=0)

    b0, w0, u0, w1, u1, u2 = (col(n) for n in range(6))
    beta_one = jnp.sqrt(add(b0 * b0) + EPS)
    inv_one = 1.0 / beta_one
    b0 = b0 * inv_one
    w0, w1 = w0 * inv_one, w1 * inv_one
    u0, u1, u2 = u0 * inv_one, u1 * inv_one, u2 * inv_one
    alpha_one = add(b0 * w0)
    x0, x1 = w0 - alpha_one * b0, w1
    beta_two = jnp.sqrt(add(x0 * x0 + x1 * x1) + EPS)
    inv_two = 1.0 / beta_two
    x0, x1 = x0 * inv_two, x1 * inv_two
    y0 = (u0 - alpha_one * w0) * inv_two - beta_two * b0
    y1 = (u1 - alpha_one * w1) * inv_two
    y2 = u2 * inv_two
    alpha_two = add(x0 * y0 + x1 * y1)
    y0, y1 = y0 - alpha_two * x0, y1 - alpha_two * x1
    beta_three = jnp.sqrt(add(y0 * y0 + y1 * y1 + y2 * y2) + EPS)
    first = alpha_one * alpha_one + beta_two * beta_two
    cross = beta_two * (alpha_one + alpha_two)
    second = beta_two * beta_two + alpha_two * alpha_two + beta_three * beta_three
    determinant = first * second - cross * cross
    coef_one = beta_one * (second * alpha_one - cross * beta_two) / determinant
    coef_two = beta_one * (first * beta_two - cross * alpha_one) / determinant
    v1 = b * inv_one
    v2 = (w * inv_one - alpha_one * v1) * inv_two
    cor_out[...] = coef_one * v1 + coef_two * v2
    whole.wait_send()


def kernel_krylov(*refs):
    trk, mod = lax.axis_index("trk"), lax.axis_index("mod")
    me = trk * 8 + mod
    barrier = pltpu.get_barrier_semaphore()

    def greet(k, carry):
        other = lax.rem(me + k, DEV)
        pl.semaphore_signal(
            barrier, inc=1, device_id=(other // 8, lax.rem(other, 8)), device_id_type=MESH
        )
        return carry

    lax.fori_loop(1, DEV, greet, 0)
    pl.semaphore_wait(barrier, DEV - 1)
    krylov(*refs)


VM = pl.BlockSpec(memory_space=pltpu.VMEM)


def on_device(ld, gd, me, hw, hm, hc, tr, rs, pw):
    send = pl.pallas_call(
        kernel_send,
        out_shape=jax.ShapeDtypeStruct((DEV, 24, LANE), F32),
        in_specs=[VM] * 7,
        out_specs=VM,
        scratch_shapes=[pltpu.VMEM((4, 192, LANE), F32)],
        name="fit_place",
    )(ld, jnp.transpose(gd, (1, 0, 2)), me, hw, hm, hc.reshape(1, TRACKS), tr.reshape(1, TRACKS))
    recv = lax.all_to_all(send, ("trk", "mod"), split_axis=0, concat_axis=0, tiled=True)
    off = (rs % NPAR).astype(F32).reshape(ROADS, 1)
    blocks, road_rhs = pl.pallas_call(
        kernel_assemble,
        grid=(DEV // GROUP,),
        out_shape=(
            jax.ShapeDtypeStruct((ROADS, LANE, LANE), F32),
            jax.ShapeDtypeStruct((ROADS, LANE), F32),
        ),
        in_specs=[
            pl.BlockSpec((GROUP, 24, LANE), lambda c: (c, 0, 0)),
            pl.BlockSpec((ROADS, 1), lambda c: (0, 0)),
        ],
        out_specs=(
            pl.BlockSpec((ROADS, LANE, LANE), lambda c: (0, 0, 0)),
            pl.BlockSpec((ROADS, LANE), lambda c: (0, 0)),
        ),
        scratch_shapes=[
            pltpu.VMEM((LANE, 2 * LANE), F32),
            pltpu.VMEM((LANE, 2 * LANE), F32),
            pltpu.VMEM((2, LANE, LANE), F32),
            pltpu.VMEM((ROADS * NPAR, 2 * LANE), BF16),
            pltpu.VMEM((ROAD, 2 * LANE), F32),
            pltpu.VMEM((LANE, 2 * LANE), F32),
        ],
        name="assemble",
    )(recv, off)
    prior = jnp.pad(pw.reshape(HALF, HALF), ((0, 0), (0, HALF)))
    rhs, cor = pl.pallas_call(
        kernel_krylov,
        out_shape=(jax.ShapeDtypeStruct((HALF, LANE), F32), jax.ShapeDtypeStruct((HALF, LANE), F32)),
        in_specs=[VM] * 4,
        out_specs=(VM, VM),
        scratch_shapes=[
            pltpu.VMEM((72, LANE), F32),
            pltpu.VMEM((3, 72, LANE), F32),
            pltpu.VMEM((72, LANE), F32),
            pltpu.VMEM((ROADS, LANE), F32),
            pltpu.VMEM((3, 8, LANE), F32),
            pltpu.VMEM((3, 8, LANE), F32),
            pltpu.VMEM((3, 8, LANE), F32),
            pltpu.VMEM((3, 8, LANE), F32),
            pltpu.VMEM((1, LANE), F32),
            pltpu.VMEM((DEV, 1, LANE), F32),
            pltpu.SemaphoreType.DMA((3, 4)),
            pltpu.SemaphoreType.DMA((2,)),
        ],
        compiler_params=pltpu.CompilerParams(collective_id=0, has_side_effects=True),
        name="krylov",
    )(blocks, road_rhs, off, prior)
    return (
        blocks,
        rhs[:, :HALF].reshape(TRACKS, NPAR),
        cor[:, :HALF].reshape(TRACKS, NPAR),
    )


def solution(mesh):
    both = ("trk", "mod")
    in_specs = (
        P(None, None, both),
        P(None, None, both),
        P(None, both),
        P(None, both),
        P(None, both),
        P(both),
        P(both),
        P(both),
        P(both, None),
    )
    out_specs = (P(both, None, None), P(both, None), P(both, None))
    return jax.shard_map(on_device, mesh=mesh, in_specs=in_specs, out_specs=out_specs, check_vma=False)
```

```python
import functools

import jax
import jax.numpy as jnp
from jax import lax
from jax.experimental import pallas as pl
from jax.experimental.pallas import tpu as pltpu
from jax.sharding import PartitionSpec as P

F32 = jnp.float32
BF16 = jnp.bfloat16
NPAR = 8
NLOC = 5
NHIT = 12
ROAD = 16
CAP = 16
LANE = 128
NMOD = 65536
ROADS = 64
TRACKS = 512
DEV = 128
GROUP = 16
PLACED = 32
EPS = 1e-6
MESH = pl.DeviceIdType.MESH
CONTRACT_LANES = (((1,), (1,)), ((), ()))


def dot_t(a, b):
    return lax.dot_general(a, b, CONTRACT_LANES, preferred_element_type=F32)


def split(x):
    hi = x.astype(BF16)
    return hi, (x - hi.astype(F32)).astype(BF16)


def fit_and_place(ld, gd, me, hw, hm, hc, tr, send, lay):
    position = lax.broadcasted_iota(jnp.int32, (NHIT, TRACKS), 0)
    live = position < hc[...]
    root = jnp.where(live, jnp.sqrt(hw[...]), 0.0)
    scaled = [ld[a] * root for a in range(NLOC)]
    factor = {}
    for i in range(NLOC):
        for j in range(i + 1):
            running = jnp.sum(scaled[i] * scaled[j], axis=0, keepdims=True)
            if i == j:
                running = running + 1.0
            for k in range(j):
                running = running - factor[i, k] * factor[j, k]
            factor[i, j] = jnp.sqrt(running) if i == j else running / factor[j, j]
    proj = []
    for i in range(NLOC):
        running = scaled[i]
        for j in range(i):
            running = running - factor[i, j] * proj[j]
        proj.append(running / factor[i, i])
    resid = me[...] * root
    solved = resid
    for a in range(NLOC):
        solved = solved - proj[a] * jnp.sum(proj[a] * resid, axis=0, keepdims=True)
    road = tr[...]
    rel = lax.rem(hm[...] - NPAR * road + NMOD, NMOD).astype(F32)
    local_road = jnp.broadcast_to((road & (ROADS - 1)).astype(F32), (NHIT, TRACKS))
    words = proj + [solved, rel, local_road]
    for c in range(TRACKS // LANE):
        at = slice(c * LANE, (c + 1) * LANE)
        for i in range(NHIT):
            lay[c, 16 * i : 16 * i + 8, :] = gd[i, :, at] * root[i : i + 1, at]
        for w, value in enumerate(words):
            lay[c, pl.ds(8 + w, 8, stride=16), :] = value[:8, at]
            lay[c, pl.ds(LANE + 8 + w, 4, stride=16), :] = value[8:, at]
    whole = jnp.concatenate([lay[c] for c in range(TRACKS // LANE)], axis=1)
    tail = whole[LANE:]
    none = jnp.zeros_like(tail)

    def both(value):
        return jnp.concatenate(split(value), axis=0)

    first_w = both(whole[:LANE])
    left_w = both(jnp.concatenate([tail, none], axis=0))
    right_w = both(jnp.concatenate([none, tail], axis=0))

    owner = road >> 6
    mine = lax.broadcasted_iota(jnp.int32, (DEV, TRACKS), 0) == owner
    member = jnp.where(mine, 1.0, 0.0)
    earlier = lax.broadcasted_iota(jnp.int32, (TRACKS, TRACKS), 0) <= lax.broadcasted_iota(
        jnp.int32, (TRACKS, TRACKS), 1
    )
    running = jnp.dot(
        member.astype(BF16), jnp.where(earlier, 1.0, 0.0).astype(BF16), preferred_element_type=F32
    )
    rank = jnp.sum(member * running, axis=0, keepdims=True) - 1.0
    slot = owner * CAP + rank.astype(jnp.int32)

    def place(step, carry):
        row = lax.broadcasted_iota(jnp.int32, (PLACED * CAP, TRACKS), 0) + step * (PLACED * CAP)
        chosen = jnp.where(row == slot, 1.0, 0.0)
        halves = chosen.reshape(PLACED, 2, 8, TRACKS)
        low = halves[:, 0].reshape(PLACED * 8, TRACKS).astype(BF16)
        high = halves[:, 1].reshape(PLACED * 8, TRACKS).astype(BF16)
        first = dot_t(chosen.astype(BF16), first_w)
        last = dot_t(low, left_w) + dot_t(high, right_w)
        at = pl.ds(pl.multiple_of(step * PLACED, PLACED), PLACED)
        send[at, 0:16, :] = (first[:, :LANE] + first[:, LANE:]).reshape(PLACED, CAP, LANE)
        send[at, 16:24, :] = (last[:, :LANE] + last[:, LANE:]).reshape(PLACED, 8, LANE)
        return carry

    lax.fori_loop(0, DEV // PLACED, place, 0)


def assemble(x, off, blocks, road_rhs, g_ref, t_ref, x_ref, hot_ref, mix_ref, z_ref):
    t0 = x[:, 0:8, :].reshape(LANE, LANE).T
    t1 = x[:, 8:16, :].reshape(LANE, LANE).T
    t2 = x[:, 16:24, :].reshape(LANE, LANE).T
    body = jnp.concatenate([t0, t1], axis=1)
    tail = jnp.concatenate([t2[:64], t2[64:]], axis=1)
    hits = []
    for i in range(NHIT):
        source, row = (body, 16 * i) if i < 8 else (tail, 16 * (i - 8))
        hits.append((source[row : row + 8], source[row + 8 : row + 16]))
    wide = 2 * LANE
    road = hits[0][1][7:8]
    each = lax.broadcasted_iota(jnp.int32, (ROADS, wide), 0).astype(F32)
    hot = jnp.where(each == road, 1.0, 0.0)
    start = jnp.sum(hot * off, axis=0, keepdims=True)
    rows = (lax.broadcasted_iota(jnp.int32, (ROADS * NPAR, wide), 0) >> 3).astype(F32)
    hot_ref[...] = jnp.where(rows == road, 1.0, 0.0).astype(BF16)
    slots = [jnp.broadcast_to(hits[i][1][6:7] - start, (8, wide)) for i in range(NHIT)]
    sums = []
    for s in range(ROAD):
        g = jnp.zeros((8, wide), F32)
        a = jnp.zeros((8, wide), F32)
        for i in range(NHIT):
            same = slots[i] == float(s)
            g = jnp.where(same, hits[i][0], g)
            a = jnp.where(same, hits[i][1], a)
        g_ref[8 * s : 8 * s + 8, :] = g
        t_ref[8 * s : 8 * s + 8, :] = 2.0 * g - g.astype(BF16).astype(F32)
        x_ref[0, 8 * s : 8 * s + 8, :] = a[:, :LANE]
        x_ref[1, 8 * s : 8 * s + 8, :] = a[:, LANE:]
        sums.append(g * a[5:6])
    v_hi, v_lo = split(jnp.concatenate(sums, axis=0))
    hot16 = hot.astype(BF16)
    road_rhs[...] += dot_t(hot16, v_hi) + dot_t(hot16, v_lo)
    lines = [
        jnp.concatenate(
            [x_ref[c, pl.ds(a, ROAD, stride=8), :] for c in range(2)], axis=1
        )
        for a in range(NLOC)
    ]

    def slot_step(s, carry):
        at = pl.ds(pl.multiple_of(s * 8, 8), 8)
        g_s = g_ref[at, :]
        a_s = jnp.concatenate([x_ref[0, at, :], x_ref[1, at, :]], axis=1)
        mix = jnp.where(lax.broadcasted_iota(jnp.int32, (ROAD, wide), 0) == s, 1.0, 0.0)
        for a in range(NLOC):
            mix = mix - a_s[a : a + 1] * lines[a]
        mix_ref[...] = mix
        for u in range(ROAD):
            z = t_ref[8 * u : 8 * u + 8, :] * mix_ref[u : u + 1, :]
            z_ref[8 * u : 8 * u + 8, :] = z
        z_both = jnp.concatenate(split(z_ref[...]), axis=0)
        g_hi = jnp.concatenate([g_s, g_s], axis=0).astype(BF16)
        hot = hot_ref[...].reshape(ROADS // 2, 16, wide)
        left = (hot * g_hi[None]).reshape(ROADS * NPAR, wide)
        out = dot_t(left, z_both)
        blocks[:, at, :] += (out[:, :LANE] + out[:, LANE:]).reshape(ROADS, NPAR, LANE)
        return carry

    lax.fori_loop(0, ROAD, slot_step, 0, unroll=2)


def symmetric(blocks):
    def one(r, carry):
        block = blocks[r]
        blocks[r] = 0.5 * (block + block.T)
        return carry

    lax.fori_loop(0, ROADS, one, 0, unroll=4)


HALF = 64


def low_lanes(x):
    return jnp.where(lax.broadcasted_iota(jnp.int32, x.shape, 1) < HALF, x, 0.0)


def spread(pieces, off, field):
    wide = jnp.concatenate([pieces, jnp.zeros_like(pieces)], axis=1)
    moved = jnp.where(off == 0.0, wide, 0.0)
    for d in range(1, NPAR):
        moved = jnp.where(off == float(d), pltpu.roll(wide, 8 * d, 1), moved)
    head, rest = moved[:, :LANE], moved[:, LANE:]
    field[...] = jnp.zeros_like(field)
    field[0:64, :] = low_lanes(head)
    field[1:65, :] += low_lanes(pltpu.roll(head, HALF, 1))
    field[2:66, :] += low_lanes(rest)


def gather(field, off):
    head = field[0:64, :] + pltpu.roll(field[1:65, :], HALF, 1)
    wide = jnp.concatenate([head, field[2:66, :]], axis=1)
    piece = jnp.where(off == 0.0, wide, 0.0)
    for d in range(1, NPAR):
        piece = jnp.where(off == float(d), pltpu.roll(wide, 2 * LANE - 8 * d, 1), piece)
    return piece[:, :LANE]


def total(x):
    return jnp.sum(jnp.sum(x, axis=0, keepdims=True), axis=1, keepdims=True)


def to_rows(x, flat):
    for c in range(TRACKS // LANE):
        block = jnp.concatenate([x[:, c * LANE : (c + 1) * LANE], jnp.zeros((LANE - NPAR, LANE), F32)], axis=0)
        flat[c * LANE : (c + 1) * LANE, :] = block.T
    rows = flat[pl.ds(0, HALF, stride=8), :]
    for m in range(1, NPAR):
        rows = rows + pltpu.roll(flat[pl.ds(m, HALF, stride=8), :], 8 * m, 1)
    return rows


def from_rows(rows, flat):
    flat[pl.ds(0, HALF, stride=8), :] = rows
    for m in range(1, NPAR):
        flat[pl.ds(m, HALF, stride=8), :] = pltpu.roll(rows, LANE - 8 * m, 1)
    return jnp.concatenate(
        [flat[c * LANE : (c + 1) * LANE, :].T[:NPAR] for c in range(TRACKS // LANE)], axis=1
    )


def position():
    return lax.axis_index("trk"), lax.axis_index("mod")


def place_of(d):
    return (d // 8, lax.rem(d, 8))


def chunk_target(n, trk, mod):
    c, j = n // GROUP, lax.rem(n, GROUP)
    m = lax.rem(c + j, 8)
    z, y = lax.rem(trk // 4 + j // 4, 4), lax.rem(lax.rem(trk, 4) + lax.rem(j, 4), 4)
    x, core = lax.rem(mod // 2 + m // 2, 4), lax.rem(mod + m, 2)
    return z * 4 + y, x * 2 + core


def kernel_all(ld, gd, me_ref, hw, hm, hc, tr, rs, pw, blocks_out, rhs_out, cor_out,
               send, recv, lay, blocks, road_rhs, g_ref, t_ref, x_ref, hot_ref, mix_ref, z_ref,
               field, vec, mapped, prior, flat, up, down, from_prev, from_next, line, lines,
               send_sem, recv_sem, rim_sem, line_sem, out_sem):
    trk, mod = position()
    me = trk * 8 + mod
    barrier = pltpu.get_barrier_semaphore()

    def greet(k, carry):
        pl.semaphore_signal(barrier, inc=1, device_id=place_of(lax.rem(me + k, DEV)), device_id_type=MESH)
        return carry

    lax.fori_loop(1, DEV, greet, 0)
    fit_and_place(ld, gd, me_ref, hw, hm, hc, tr, send, lay)
    pl.semaphore_wait(barrier, DEV - 1)

    own = pltpu.make_async_copy(send.at[me], recv.at[0], recv_sem.at[0])
    own.start()

    def send_chunk(n, carry):
        t, m = chunk_target(n, trk, mod)
        pltpu.make_async_remote_copy(
            send.at[t * 8 + m], recv.at[n], send_sem, recv_sem.at[n // GROUP], device_id=(t, m), device_id_type=MESH
        ).start()
        return carry

    lax.fori_loop(1, DEV, send_chunk, 0)

    start = lax.rem(rs[...], NPAR).astype(F32)
    diagonal = lax.broadcasted_iota(jnp.int32, (ROADS, ROADS), 0) == lax.broadcasted_iota(
        jnp.int32, (ROADS, ROADS), 1
    )
    off = jnp.sum(jnp.where(diagonal, start, 0.0), axis=1, keepdims=True)
    prior[...] = to_rows(pw[...], flat)
    blocks[...] = jnp.zeros_like(blocks)
    road_rhs[...] = jnp.zeros_like(road_rhs)

    def take_group(c, carry):
        at = pl.ds(pl.multiple_of(c * GROUP, GROUP), GROUP)
        pltpu.make_async_copy(recv.at[at], recv.at[at], recv_sem.at[c]).wait()
        assemble(recv[at], off, blocks, road_rhs, g_ref, t_ref, x_ref, hot_ref, mix_ref, z_ref)
        return carry

    lax.fori_loop(0, DEV // GROUP, take_group, 0)

    nxt = lax.rem(me + 1, DEV)
    prv = lax.rem(me + DEV - 1, DEV)
    out_copy = pltpu.make_async_copy(blocks, blocks_out, out_sem)

    def exchange(e, target, between):
        up[e] = field[64:72, :]
        down[e] = field[0:8, :]
        to_next = pltpu.make_async_remote_copy(
            up.at[e], from_prev.at[e], rim_sem.at[e, 0], rim_sem.at[e, 1], device_id=place_of(nxt), device_id_type=MESH
        )
        to_prev = pltpu.make_async_remote_copy(
            down.at[e], from_next.at[e], rim_sem.at[e, 2], rim_sem.at[e, 3], device_id=place_of(prv), device_id_type=MESH
        )
        to_next.start()
        to_prev.start()
        target[8:64, :] = field[8:64, :]
        between()
        to_next.wait()
        to_prev.wait()
        keep = lax.broadcasted_iota(jnp.int32, (8, LANE), 0) < 2
        target[0:8, :] = field[0:8, :] + jnp.where(keep, from_prev[e], 0.0)
        target[64:72, :] = jnp.where(keep, field[64:72, :] + from_next[e], 0.0)

    def apply(source, e, target, between):
        flipped = gather(source, off).T
        for r in range(ROADS):
            mapped[r : r + 1, :] = jnp.sum(blocks[r] * flipped[:, r : r + 1], axis=0, keepdims=True)
        spread(mapped[...], off, field)
        field[0:64, :] += prior[...] * source[0:64, :]
        exchange(e, target, between)

    def finish_blocks():
        symmetric(blocks)
        out_copy.start()

    def give_rhs():
        rhs_out[...] = from_rows(vec[0, 0:64, :], flat)

    def nothing():
        pass

    spread(road_rhs[...], off, field)
    exchange(0, vec.at[0], finish_blocks)
    apply(vec.at[0], 1, vec.at[1], give_rhs)
    apply(vec.at[1], 2, vec.at[2], nothing)
    b, w, u = vec[0, 0:64, :], vec[1, 0:64, :], vec[2, 0:64, :]

    def unit(norm):
        return jnp.where(norm > 0.0, 1.0 / jnp.where(norm > 0.0, norm, 1.0), 0.0)

    r11 = jnp.sqrt(total(b * b))
    q1 = b * unit(r11)
    r12 = total(q1 * w)
    r13 = total(q1 * u)
    w1 = w - r12 * q1
    u1 = u - r13 * q1
    r22 = jnp.sqrt(total(w1 * w1))
    q2 = w1 * unit(r22)
    r23 = total(q2 * u1)
    u2 = u1 - r23 * q2
    r33 = jnp.sqrt(total(u2 * u2))
    lane = lax.broadcasted_iota(jnp.int32, (1, LANE), 1)
    row = jnp.zeros((1, LANE), F32)
    for n, value in enumerate((r11, r12, r13, r22, r23, r33)):
        row = jnp.where(lane == n, value, row)
    line[...] = row
    lines[me] = row

    def send_line(k, carry):
        pltpu.make_async_remote_copy(
            line, lines.at[me], line_sem.at[0], line_sem.at[1],
            device_id=place_of(lax.rem(me + k, DEV)), device_id_type=MESH,
        ).start()
        return carry

    lax.fori_loop(1, DEV, send_line, 0)
    w8 = from_rows(w, flat)
    whole = pltpu.make_async_remote_copy(
        lines.at[pl.ds(0, DEV - 1)], lines.at[pl.ds(0, DEV - 1)], line_sem.at[0], line_sem.at[1],
        device_id=place_of(nxt), device_id_type=MESH,
    )
    whole.wait_recv()
    every = lines[...]

    def col(n):
        return every[:, :, n : n + 1]

    def add(x):
        return jnp.sum(x, axis=0)

    b0, w0, u0, w1, u1, u2 = (col(n) for n in range(6))
    beta_one = jnp.sqrt(add(b0 * b0) + EPS)
    inv_one = 1.0 / beta_one
    b0 = b0 * inv_one
    w0, w1 = w0 * inv_one, w1 * inv_one
    u0, u1, u2 = u0 * inv_one, u1 * inv_one, u2 * inv_one
    alpha_one = add(b0 * w0)
    x0, x1 = w0 - alpha_one * b0, w1
    beta_two = jnp.sqrt(add(x0 * x0 + x1 * x1) + EPS)
    inv_two = 1.0 / beta_two
    x0, x1 = x0 * inv_two, x1 * inv_two
    y0 = (u0 - alpha_one * w0) * inv_two - beta_two * b0
    y1 = (u1 - alpha_one * w1) * inv_two
    y2 = u2 * inv_two
    alpha_two = add(x0 * y0 + x1 * y1)
    y0, y1 = y0 - alpha_two * x0, y1 - alpha_two * x1
    beta_three = jnp.sqrt(add(y0 * y0 + y1 * y1 + y2 * y2) + EPS)
    first = alpha_one * alpha_one + beta_two * beta_two
    cross = beta_two * (alpha_one + alpha_two)
    second = beta_two * beta_two + alpha_two * alpha_two + beta_three * beta_three
    determinant = first * second - cross * cross
    coef_one = beta_one * (second * alpha_one - cross * beta_two) / determinant
    coef_two = beta_one * (first * beta_two - cross * alpha_one) / determinant
    v1 = rhs_out[...] * inv_one
    v2 = (w8 * inv_one - alpha_one * v1) * inv_two
    cor_out[...] = coef_one * v1 + coef_two * v2
    whole.wait_send()
    sent = pltpu.make_async_remote_copy(
        send.at[pl.ds(0, DEV - 1)], recv.at[pl.ds(0, DEV - 1)], send_sem, recv_sem.at[0],
        device_id=place_of(nxt), device_id_type=MESH,
    )
    sent.wait_send()
    out_copy.wait()


VM = pl.BlockSpec(memory_space=pltpu.VMEM)


def on_device(ld, gd, me, hw, hm, hc, tr, rs, pw):
    def vmem(*shape, dtype=F32):
        return pltpu.VMEM(shape, dtype)

    blocks, rhs, cor = pl.pallas_call(
        kernel_all,
        out_shape=(
            jax.ShapeDtypeStruct((ROADS, LANE, LANE), F32),
            jax.ShapeDtypeStruct((NPAR, TRACKS), F32),
            jax.ShapeDtypeStruct((NPAR, TRACKS), F32),
        ),
        in_specs=[VM] * 9,
        out_specs=(pl.BlockSpec(memory_space=pl.ANY), VM, VM),
        scratch_shapes=[
            vmem(DEV, 24, LANE),
            vmem(DEV, 24, LANE),
            vmem(4, 192, LANE),
            vmem(ROADS, LANE, LANE),
            vmem(ROADS, LANE),
            vmem(LANE, 2 * LANE),
            vmem(LANE, 2 * LANE),
            vmem(2, LANE, LANE),
            vmem(ROADS * NPAR, 2 * LANE, dtype=BF16),
            vmem(ROAD, 2 * LANE),
            vmem(LANE, 2 * LANE),
            vmem(72, LANE),
            vmem(3, 72, LANE),
            vmem(ROADS, LANE),
            vmem(HALF, LANE),
            vmem(TRACKS, LANE),
            vmem(3, 8, LANE),
            vmem(3, 8, LANE),
            vmem(3, 8, LANE),
            vmem(3, 8, LANE),
            vmem(1, LANE),
            vmem(DEV, 1, LANE),
            pltpu.SemaphoreType.DMA,
            pltpu.SemaphoreType.DMA((DEV // GROUP,)),
            pltpu.SemaphoreType.DMA((3, 4)),
            pltpu.SemaphoreType.DMA((2,)),
            pltpu.SemaphoreType.DMA,
        ],
        compiler_params=pltpu.CompilerParams(collective_id=0, has_side_effects=True),
        name="alignment",
    )(
        ld,
        jnp.transpose(gd, (1, 0, 2)),
        me,
        hw,
        hm,
        hc.reshape(1, TRACKS),
        tr.reshape(1, TRACKS),
        rs.reshape(1, ROADS),
        pw.T,
    )
    return blocks, rhs.T, cor.T


def solution(mesh):
    both = ("trk", "mod")
    in_specs = (
        P(None, None, both),
        P(None, None, both),
        P(None, both),
        P(None, both),
        P(None, both),
        P(both),
        P(both),
        P(both),
        P(both, None),
    )
    out_specs = (P(both, None, None), P(both, None), P(both, None))
    return jax.shard_map(on_device, mesh=mesh, in_specs=in_specs, out_specs=out_specs, check_vma=False)
```

```python
import functools

import jax
import jax.numpy as jnp
from jax import lax
from jax.experimental import pallas as pl
from jax.experimental.pallas import tpu as pltpu
from jax.sharding import PartitionSpec as P

F32 = jnp.float32
BF16 = jnp.bfloat16
NPAR = 8
NLOC = 5
NHIT = 12
ROAD = 16
CAP = 16
LANE = 128
NMOD = 65536
ROADS = 64
TRACKS = 512
DEV = 128
GROUP = 16
PLACED = 32
EPS = 1e-6
MESH = pl.DeviceIdType.MESH
CONTRACT_LANES = (((1,), (1,)), ((), ()))


def dot_t(a, b):
    return lax.dot_general(a, b, CONTRACT_LANES, preferred_element_type=F32)


def split(x):
    hi = x.astype(BF16)
    return hi, (x - hi.astype(F32)).astype(BF16)


def fit_and_place(ld, gd, me, hw, hm, hc, tr, send, lay, trk, mod, ready):
    position = lax.broadcasted_iota(jnp.int32, (NHIT, TRACKS), 0)
    live = position < hc[...]
    root = jnp.where(live, jnp.sqrt(hw[...]), 0.0)
    scaled = [ld[a] * root for a in range(NLOC)]
    factor = {}
    for i in range(NLOC):
        for j in range(i + 1):
            running = jnp.sum(scaled[i] * scaled[j], axis=0, keepdims=True)
            if i == j:
                running = running + 1.0
            for k in range(j):
                running = running - factor[i, k] * factor[j, k]
            factor[i, j] = jnp.sqrt(running) if i == j else running / factor[j, j]
    proj = []
    for i in range(NLOC):
        running = scaled[i]
        for j in range(i):
            running = running - factor[i, j] * proj[j]
        proj.append(running / factor[i, i])
    resid = me[...] * root
    solved = resid
    for a in range(NLOC):
        solved = solved - proj[a] * jnp.sum(proj[a] * resid, axis=0, keepdims=True)
    road = tr[...]
    rel = lax.rem(hm[...] - NPAR * road + NMOD, NMOD).astype(F32)
    local_road = jnp.broadcast_to((road & (ROADS - 1)).astype(F32), (NHIT, TRACKS))
    words = proj + [solved, rel, local_road]
    for c in range(TRACKS // LANE):
        at = slice(c * LANE, (c + 1) * LANE)
        for i in range(NHIT):
            lay[c, 16 * i : 16 * i + 8, :] = gd[i, :, at] * root[i : i + 1, at]
        for w, value in enumerate(words):
            lay[c, pl.ds(8 + w, 8, stride=16), :] = value[:8, at]
            lay[c, pl.ds(LANE + 8 + w, 4, stride=16), :] = value[8:, at]
    whole = jnp.concatenate([lay[c] for c in range(TRACKS // LANE)], axis=1)
    tail = whole[LANE:]
    none = jnp.zeros_like(tail)

    def both(value):
        return jnp.concatenate(split(value), axis=0)

    first_w = both(whole[:LANE])
    left_w = both(jnp.concatenate([tail, none], axis=0))
    right_w = both(jnp.concatenate([none, tail], axis=0))

    owner = road >> 6
    z, y, x, core = trk // 4, lax.rem(trk, 4), mod // 2, lax.rem(mod, 2)
    j = (((owner >> 5) - z) & 3) * 4 + (((owner >> 3) - y) & 3)
    m = (((owner >> 1) - x) & 3) * 2 + ((owner - core) & 1)
    chunk = ((m - j) & 7) * GROUP + j
    member = jnp.where(lax.broadcasted_iota(jnp.int32, (DEV, TRACKS), 0) == chunk, 1.0, 0.0)
    earlier = lax.broadcasted_iota(jnp.int32, (TRACKS, TRACKS), 0) <= lax.broadcasted_iota(
        jnp.int32, (TRACKS, TRACKS), 1
    )
    running = jnp.dot(
        member.astype(BF16), jnp.where(earlier, 1.0, 0.0).astype(BF16), preferred_element_type=F32
    )
    rank = jnp.sum(member * running, axis=0, keepdims=True) - 1.0
    slot = chunk * CAP + rank.astype(jnp.int32)

    for step in range(DEV // PLACED):
        row = lax.broadcasted_iota(jnp.int32, (PLACED * CAP, TRACKS), 0) + step * (PLACED * CAP)
        chosen = jnp.where(row == slot, 1.0, 0.0)
        halves = chosen.reshape(PLACED, 2, 8, TRACKS)
        low = halves[:, 0].reshape(PLACED * 8, TRACKS).astype(BF16)
        high = halves[:, 1].reshape(PLACED * 8, TRACKS).astype(BF16)
        first = dot_t(chosen.astype(BF16), first_w)
        last = dot_t(low, left_w) + dot_t(high, right_w)
        at = slice(step * PLACED, (step + 1) * PLACED)
        send[at, 0:16, :] = (first[:, :LANE] + first[:, LANE:]).reshape(PLACED, CAP, LANE)
        send[at, 16:24, :] = (last[:, :LANE] + last[:, LANE:]).reshape(PLACED, 8, LANE)
        ready(step)


def assemble(x, off, blocks, road_rhs, g_ref, t_ref, x_ref, hot_ref, mix_ref):
    t0 = x[:, 0:8, :].reshape(LANE, LANE).T
    t1 = x[:, 8:16, :].reshape(LANE, LANE).T
    t2 = x[:, 16:24, :].reshape(LANE, LANE).T
    body = jnp.concatenate([t0, t1], axis=1)
    tail = jnp.concatenate([t2[:64], t2[64:]], axis=1)
    hits = []
    for i in range(NHIT):
        source, row = (body, 16 * i) if i < 8 else (tail, 16 * (i - 8))
        hits.append((source[row : row + 8], source[row + 8 : row + 16]))
    wide = 2 * LANE
    road = hits[0][1][7:8]
    each = lax.broadcasted_iota(jnp.int32, (ROADS, wide), 0).astype(F32)
    hot = jnp.where(each == road, 1.0, 0.0)
    start = jnp.sum(hot * off, axis=0, keepdims=True)
    rows = (lax.broadcasted_iota(jnp.int32, (ROADS * NPAR, wide), 0) >> 3).astype(F32)
    hot_ref[...] = jnp.where(rows == road, 1.0, 0.0).astype(BF16)
    slots = [jnp.broadcast_to(hits[i][1][6:7] - start, (8, wide)) for i in range(NHIT)]
    sums = []
    for s in range(ROAD):
        g = jnp.zeros((8, wide), F32)
        a = jnp.zeros((8, wide), F32)
        for i in range(NHIT):
            same = slots[i] == float(s)
            g = jnp.where(same, hits[i][0], g)
            a = jnp.where(same, hits[i][1], a)
        g_ref[8 * s : 8 * s + 8, :] = g
        t_ref[8 * s : 8 * s + 8, :] = 2.0 * g - g.astype(BF16).astype(F32)
        x_ref[0, 8 * s : 8 * s + 8, :] = a[:, :LANE]
        x_ref[1, 8 * s : 8 * s + 8, :] = a[:, LANE:]
        sums.append(g * a[5:6])
    v_hi, v_lo = split(jnp.concatenate(sums, axis=0))
    hot16 = hot.astype(BF16)
    road_rhs[...] += dot_t(hot16, v_hi) + dot_t(hot16, v_lo)
    lines = [
        jnp.concatenate(
            [x_ref[c, pl.ds(a, ROAD, stride=8), :] for c in range(2)], axis=1
        )
        for a in range(NLOC)
    ]

    ident = lax.broadcasted_iota(jnp.int32, (ROAD, wide), 0)
    for s in range(ROAD):
        mix = jnp.where(ident == s, 1.0, 0.0)
        for a in range(NLOC):
            mix = mix - lines[a][s : s + 1] * lines[a]
        mix_ref[ROAD * s : ROAD * s + ROAD, :] = mix

    for s in range(ROAD):
        at = slice(8 * s, 8 * s + 8)
        z = jnp.concatenate(
            [
                t_ref[8 * u : 8 * u + 8, :] * mix_ref[ROAD * s + u : ROAD * s + u + 1, :]
                for u in range(ROAD)
            ],
            axis=0,
        )
        z_both = jnp.concatenate(split(z), axis=0)
        g_s = g_ref[at, :]
        g_hi = jnp.concatenate([g_s, g_s], axis=0).astype(BF16)
        hot = hot_ref[...].reshape(ROADS // 2, 16, wide)
        left = (hot * g_hi[None]).reshape(ROADS * NPAR, wide)
        out = dot_t(left, z_both)
        blocks[:, at, :] += (out[:, :LANE] + out[:, LANE:]).reshape(ROADS, NPAR, LANE)


def symmetric(blocks):
    def one(r, carry):
        block = blocks[r]
        blocks[r] = 0.5 * (block + block.T)
        return carry

    lax.fori_loop(0, ROADS, one, 0, unroll=4)


HALF = 64


def low_lanes(x):
    return jnp.where(lax.broadcasted_iota(jnp.int32, x.shape, 1) < HALF, x, 0.0)


def spread(pieces, off, field):
    wide = jnp.concatenate([pieces, jnp.zeros_like(pieces)], axis=1)
    moved = jnp.where(off == 0.0, wide, 0.0)
    for d in range(1, NPAR):
        moved = jnp.where(off == float(d), pltpu.roll(wide, 8 * d, 1), moved)
    head, rest = moved[:, :LANE], moved[:, LANE:]
    field[...] = jnp.zeros_like(field)
    field[0:64, :] = low_lanes(head)
    field[1:65, :] += low_lanes(pltpu.roll(head, HALF, 1))
    field[2:66, :] += low_lanes(rest)


def gather(field, off):
    head = field[0:64, :] + pltpu.roll(field[1:65, :], HALF, 1)
    wide = jnp.concatenate([head, field[2:66, :]], axis=1)
    piece = jnp.where(off == 0.0, wide, 0.0)
    for d in range(1, NPAR):
        piece = jnp.where(off == float(d), pltpu.roll(wide, 2 * LANE - 8 * d, 1), piece)
    return piece[:, :LANE]


def total(x):
    return jnp.sum(jnp.sum(x, axis=0, keepdims=True), axis=1, keepdims=True)


def to_rows(x, flat):
    for c in range(TRACKS // LANE):
        block = jnp.concatenate([x[:, c * LANE : (c + 1) * LANE], jnp.zeros((LANE - NPAR, LANE), F32)], axis=0)
        flat[c * LANE : (c + 1) * LANE, :] = block.T
    rows = flat[pl.ds(0, HALF, stride=8), :]
    for m in range(1, NPAR):
        rows = rows + pltpu.roll(flat[pl.ds(m, HALF, stride=8), :], 8 * m, 1)
    return rows


def from_rows(rows, flat):
    flat[pl.ds(0, HALF, stride=8), :] = rows
    for m in range(1, NPAR):
        flat[pl.ds(m, HALF, stride=8), :] = pltpu.roll(rows, LANE - 8 * m, 1)
    return jnp.concatenate(
        [flat[c * LANE : (c + 1) * LANE, :].T[:NPAR] for c in range(TRACKS // LANE)], axis=1
    )


def position():
    return lax.axis_index("trk"), lax.axis_index("mod")


def place_of(d):
    return (d // 8, lax.rem(d, 8))


def kernel_all(ld, gd, me_ref, hw, hm, hc, tr, rs, pw, blocks_out, rhs_out, cor_out,
               send, recv, lay, blocks, road_rhs, g_ref, t_ref, x_ref, hot_ref, mix_ref,
               field, vec, mapped, prior, flat, up, down, from_prev, from_next, line, lines,
               send_sem, recv_sem, rim_sem, line_sem, out_sem):
    trk, mod = position()
    me = trk * 8 + mod
    barrier = pltpu.get_barrier_semaphore()

    z, y, x, core = trk // 4, lax.rem(trk, 4), mod // 2, lax.rem(mod, 2)
    zs = [lax.rem(z + d, 4) * 4 for d in range(4)]
    ys = [lax.rem(y + d, 4) for d in range(4)]
    xs = [lax.rem(x + d, 4) * 2 for d in range(4)]
    cores = [core, 1 - core]
    trks = [zs[j // 4] + ys[j % 4] for j in range(GROUP)]
    mods = [xs[m // 2] + cores[m % 2] for m in range(8)]
    others = [(trks[j], mods[m]) for m in range(8) for j in range(GROUP) if j or m]
    for other in others:
        pl.semaphore_signal(barrier, inc=1, device_id=other, device_id_type=MESH)
    own = pltpu.make_async_copy(send.at[0], recv.at[0], recv_sem.at[0])

    def ready(step):
        if step == 0:
            pl.semaphore_wait(barrier, DEV - 1)
            own.start()
        for n in range(max(1, step * PLACED), (step + 1) * PLACED):
            c, j = n // GROUP, n % GROUP
            pltpu.make_async_remote_copy(
                send.at[n], recv.at[n], send_sem, recv_sem.at[c],
                device_id=(trks[j], mods[(c + j) % 8]), device_id_type=MESH,
            ).start()

    fit_and_place(ld, gd, me_ref, hw, hm, hc, tr, send, lay, trk, mod, ready)

    start = lax.rem(rs[...], NPAR).astype(F32)
    diagonal = lax.broadcasted_iota(jnp.int32, (ROADS, ROADS), 0) == lax.broadcasted_iota(
        jnp.int32, (ROADS, ROADS), 1
    )
    off = jnp.sum(jnp.where(diagonal, start, 0.0), axis=1, keepdims=True)
    prior[...] = to_rows(pw[...], flat)
    blocks[...] = jnp.zeros_like(blocks)
    road_rhs[...] = jnp.zeros_like(road_rhs)

    def take_group(c, carry):
        at = pl.ds(pl.multiple_of(c * GROUP, GROUP), GROUP)
        pltpu.make_async_copy(recv.at[at], recv.at[at], recv_sem.at[c]).wait()
        assemble(recv[at], off, blocks, road_rhs, g_ref, t_ref, x_ref, hot_ref, mix_ref)
        return carry

    lax.fori_loop(0, DEV // GROUP, take_group, 0)

    nxt = lax.rem(me + 1, DEV)
    prv = lax.rem(me + DEV - 1, DEV)
    out_copy = pltpu.make_async_copy(blocks, blocks_out, out_sem)

    def exchange(e, target, between):
        up[e] = field[64:72, :]
        down[e] = field[0:8, :]
        to_next = pltpu.make_async_remote_copy(
            up.at[e], from_prev.at[e], rim_sem.at[e, 0], rim_sem.at[e, 1], device_id=place_of(nxt), device_id_type=MESH
        )
        to_prev = pltpu.make_async_remote_copy(
            down.at[e], from_next.at[e], rim_sem.at[e, 2], rim_sem.at[e, 3], device_id=place_of(prv), device_id_type=MESH
        )
        to_next.start()
        to_prev.start()
        target[8:64, :] = field[8:64, :]
        between()
        to_next.wait()
        to_prev.wait()
        keep = lax.broadcasted_iota(jnp.int32, (8, LANE), 0) < 2
        target[0:8, :] = field[0:8, :] + jnp.where(keep, from_prev[e], 0.0)
        target[64:72, :] = jnp.where(keep, field[64:72, :] + from_next[e], 0.0)

    def apply(source, e, target, between):
        flipped = gather(source, off).T
        for r in range(ROADS):
            mapped[r : r + 1, :] = jnp.sum(blocks[r] * flipped[:, r : r + 1], axis=0, keepdims=True)
        spread(mapped[...], off, field)
        field[0:64, :] += prior[...] * source[0:64, :]
        exchange(e, target, between)

    def finish_blocks():
        symmetric(blocks)
        out_copy.start()

    def give_rhs():
        rhs_out[...] = from_rows(vec[0, 0:64, :], flat)

    def nothing():
        pass

    spread(road_rhs[...], off, field)
    exchange(0, vec.at[0], finish_blocks)
    apply(vec.at[0], 1, vec.at[1], give_rhs)
    apply(vec.at[1], 2, vec.at[2], nothing)
    b, w, u = vec[0, 0:64, :], vec[1, 0:64, :], vec[2, 0:64, :]

    def inverse(value):
        return jnp.where(value > 0.0, 1.0 / jnp.where(value > 0.0, value, 1.0), 0.0)

    bb, bw, bu = total(b * b), total(b * w), total(b * u)
    inv_bb = inverse(bb)
    w1 = w - (bw * inv_bb) * b
    u1 = u - (bu * inv_bb) * b
    ww, wu = total(w1 * w1), total(w1 * u1)
    u2 = u1 - (wu * inverse(ww)) * w1
    uu = total(u2 * u2)
    r11, r22 = jnp.sqrt(bb), jnp.sqrt(ww)
    lane = lax.broadcasted_iota(jnp.int32, (1, LANE), 1)
    row = jnp.zeros((1, LANE), F32)
    for n, value in enumerate((r11, bw * inverse(r11), bu * inverse(r11), r22, wu * inverse(r22), jnp.sqrt(uu))):
        row = jnp.where(lane == n, value, row)
    line[...] = row
    lines[me] = row
    for other in others:
        pltpu.make_async_remote_copy(
            line, lines.at[me], line_sem.at[0], line_sem.at[1], device_id=other, device_id_type=MESH
        ).start()
    w8 = from_rows(w, flat)
    whole = pltpu.make_async_remote_copy(
        lines.at[pl.ds(0, DEV - 1)], lines.at[pl.ds(0, DEV - 1)], line_sem.at[0], line_sem.at[1],
        device_id=place_of(nxt), device_id_type=MESH,
    )
    whole.wait_recv()
    for d in range(DEV):
        flat[d : d + 1, :] = lines[d]
    every = flat[0:DEV, :].T

    def add(x):
        return jnp.sum(x, axis=1, keepdims=True)

    b0, w0, u0, w1, u1, u2 = (every[n : n + 1, :] for n in range(6))
    square = add(b0 * b0) + EPS
    alpha_one = add(b0 * w0) / square
    beta_one = jnp.sqrt(square)
    inv_one = 1.0 / beta_one
    x0, x1 = (w0 - alpha_one * b0) * inv_one, w1 * inv_one
    beta_two = jnp.sqrt(add(x0 * x0 + x1 * x1) + EPS)
    inv_two = 1.0 / beta_two
    x0, x1 = x0 * inv_two, x1 * inv_two
    both_inv = inv_one * inv_two
    y0 = (u0 - alpha_one * w0) * both_inv - beta_two * inv_one * b0
    y1 = (u1 - alpha_one * w1) * both_inv
    y2 = u2 * both_inv
    alpha_two = add(x0 * y0 + x1 * y1)
    y0, y1 = y0 - alpha_two * x0, y1 - alpha_two * x1
    beta_three = jnp.sqrt(add(y0 * y0 + y1 * y1 + y2 * y2) + EPS)
    first = alpha_one * alpha_one + beta_two * beta_two
    cross = beta_two * (alpha_one + alpha_two)
    second = beta_two * beta_two + alpha_two * alpha_two + beta_three * beta_three
    determinant = first * second - cross * cross
    coef_one = beta_one * (second * alpha_one - cross * beta_two) / determinant
    coef_two = beta_one * (first * beta_two - cross * alpha_one) / determinant
    v1 = rhs_out[...] * inv_one
    v2 = (w8 * inv_one - alpha_one * v1) * inv_two
    cor_out[...] = coef_one * v1 + coef_two * v2
    whole.wait_send()
    sent = pltpu.make_async_remote_copy(
        send.at[pl.ds(0, DEV - 1)], recv.at[pl.ds(0, DEV - 1)], send_sem, recv_sem.at[0],
        device_id=place_of(nxt), device_id_type=MESH,
    )
    sent.wait_send()
    out_copy.wait()


VM = pl.BlockSpec(memory_space=pltpu.VMEM)


def on_device(ld, gd, me, hw, hm, hc, tr, rs, pw):
    def vmem(*shape, dtype=F32):
        return pltpu.VMEM(shape, dtype)

    blocks, rhs, cor = pl.pallas_call(
        kernel_all,
        out_shape=(
            jax.ShapeDtypeStruct((ROADS, LANE, LANE), F32),
            jax.ShapeDtypeStruct((NPAR, TRACKS), F32),
            jax.ShapeDtypeStruct((NPAR, TRACKS), F32),
        ),
        in_specs=[VM] * 9,
        out_specs=(pl.BlockSpec(memory_space=pl.ANY), VM, VM),
        scratch_shapes=[
            vmem(DEV, 24, LANE),
            vmem(DEV, 24, LANE),
            vmem(4, 192, LANE),
            vmem(ROADS, LANE, LANE),
            vmem(ROADS, LANE),
            vmem(LANE, 2 * LANE),
            vmem(LANE, 2 * LANE),
            vmem(2, LANE, LANE),
            vmem(ROADS * NPAR, 2 * LANE, dtype=BF16),
            vmem(ROAD * ROAD, 2 * LANE),
            vmem(72, LANE),
            vmem(3, 72, LANE),
            vmem(ROADS, LANE),
            vmem(HALF, LANE),
            vmem(TRACKS, LANE),
            vmem(3, 8, LANE),
            vmem(3, 8, LANE),
            vmem(3, 8, LANE),
            vmem(3, 8, LANE),
            vmem(1, LANE),
            vmem(DEV, 1, LANE),
            pltpu.SemaphoreType.DMA,
            pltpu.SemaphoreType.DMA((DEV // GROUP,)),
            pltpu.SemaphoreType.DMA((3, 4)),
            pltpu.SemaphoreType.DMA((2,)),
            pltpu.SemaphoreType.DMA,
        ],
        compiler_params=pltpu.CompilerParams(collective_id=0, has_side_effects=True),
        name="alignment",
    )(
        ld,
        jnp.transpose(gd, (1, 0, 2)),
        me,
        hw,
        hm,
        hc.reshape(1, TRACKS),
        tr.reshape(1, TRACKS),
        rs.reshape(1, ROADS),
        pw.T,
    )
    return blocks, rhs.T, cor.T


def solution(mesh):
    both = ("trk", "mod")
    in_specs = (
        P(None, None, both),
        P(None, None, both),
        P(None, both),
        P(None, both),
        P(None, both),
        P(both),
        P(both),
        P(both),
        P(both, None),
    )
    out_specs = (P(both, None, None), P(both, None), P(both, None))
    return jax.shard_map(on_device, mesh=mesh, in_specs=in_specs, out_specs=out_specs, check_vma=False)
```

```python
import functools

import jax
import jax.numpy as jnp
from jax import lax
from jax.experimental import pallas as pl
from jax.experimental.pallas import tpu as pltpu
from jax.sharding import PartitionSpec as P

F32 = jnp.float32
BF16 = jnp.bfloat16
NPAR = 8
NLOC = 5
NHIT = 12
ROAD = 16
CAP = 16
LANE = 128
NMOD = 65536
ROADS = 64
TRACKS = 512
DEV = 128
GROUP = 16
PLACED = 32
EPS = 1e-6
MESH = pl.DeviceIdType.MESH
CONTRACT_LANES = (((1,), (1,)), ((), ()))


def dot_t(a, b):
    return lax.dot_general(a, b, CONTRACT_LANES, preferred_element_type=F32)


def split(x):
    hi = x.astype(BF16)
    return hi, (x - hi.astype(F32)).astype(BF16)


def fit_and_place(ld, gd, me, hw, hm, hc, tr, send, lay, trk, mod, ready):
    position = lax.broadcasted_iota(jnp.int32, (NHIT, TRACKS), 0)
    live = position < hc[...]
    root = jnp.where(live, jnp.sqrt(hw[...]), 0.0)
    scaled = [ld[a] * root for a in range(NLOC)]
    factor = {}
    for i in range(NLOC):
        for j in range(i + 1):
            running = jnp.sum(scaled[i] * scaled[j], axis=0, keepdims=True)
            if i == j:
                running = running + 1.0
            for k in range(j):
                running = running - factor[i, k] * factor[j, k]
            factor[i, j] = jnp.sqrt(running) if i == j else running / factor[j, j]
    proj = []
    for i in range(NLOC):
        running = scaled[i]
        for j in range(i):
            running = running - factor[i, j] * proj[j]
        proj.append(running / factor[i, i])
    resid = me[...] * root
    solved = resid
    for a in range(NLOC):
        solved = solved - proj[a] * jnp.sum(proj[a] * resid, axis=0, keepdims=True)
    road = tr[...]
    rel = lax.rem(hm[...] - NPAR * road + NMOD, NMOD).astype(F32)
    local_road = jnp.broadcast_to((road & (ROADS - 1)).astype(F32), (NHIT, TRACKS))
    words = proj + [solved, rel, local_road]
    for c in range(TRACKS // LANE):
        at = slice(c * LANE, (c + 1) * LANE)
        for i in range(NHIT):
            lay[c, 16 * i : 16 * i + 8, :] = gd[i, :, at] * root[i : i + 1, at]
        for w, value in enumerate(words):
            lay[c, pl.ds(8 + w, 8, stride=16), :] = value[:8, at]
            lay[c, pl.ds(LANE + 8 + w, 4, stride=16), :] = value[8:, at]
    whole = jnp.concatenate([lay[c] for c in range(TRACKS // LANE)], axis=1)
    tail = whole[LANE:]
    none = jnp.zeros_like(tail)

    def both(value):
        return jnp.concatenate(split(value), axis=0)

    first_w = both(whole[:LANE])
    left_w = both(jnp.concatenate([tail, none], axis=0))
    right_w = both(jnp.concatenate([none, tail], axis=0))

    owner = road >> 6
    z, y, x, core = trk // 4, lax.rem(trk, 4), mod // 2, lax.rem(mod, 2)
    j = (((owner >> 5) - z) & 3) * 4 + (((owner >> 3) - y) & 3)
    m = (((owner >> 1) - x) & 3) * 2 + ((owner - core) & 1)
    chunk = ((m - j) & 7) * GROUP + j
    member = jnp.where(lax.broadcasted_iota(jnp.int32, (DEV, TRACKS), 0) == chunk, 1.0, 0.0)
    earlier = lax.broadcasted_iota(jnp.int32, (TRACKS, TRACKS), 0) <= lax.broadcasted_iota(
        jnp.int32, (TRACKS, TRACKS), 1
    )
    running = jnp.dot(
        member.astype(BF16), jnp.where(earlier, 1.0, 0.0).astype(BF16), preferred_element_type=F32
    )
    rank = jnp.sum(member * running, axis=0, keepdims=True) - 1.0
    slot = chunk * CAP + rank.astype(jnp.int32)

    for step in range(DEV // PLACED):
        row = lax.broadcasted_iota(jnp.int32, (PLACED * CAP, TRACKS), 0) + step * (PLACED * CAP)
        chosen = jnp.where(row == slot, 1.0, 0.0)
        halves = chosen.reshape(PLACED, 2, 8, TRACKS)
        low = halves[:, 0].reshape(PLACED * 8, TRACKS).astype(BF16)
        high = halves[:, 1].reshape(PLACED * 8, TRACKS).astype(BF16)
        first = dot_t(chosen.astype(BF16), first_w)
        last = dot_t(low, left_w) + dot_t(high, right_w)
        at = slice(step * PLACED, (step + 1) * PLACED)
        send[at, 0:16, :] = (first[:, :LANE] + first[:, LANE:]).reshape(PLACED, CAP, LANE)
        send[at, 16:24, :] = (last[:, :LANE] + last[:, LANE:]).reshape(PLACED, 8, LANE)
        ready(step)


def assemble(x, off, blocks, road_rhs, g_ref, t_ref, x_ref, hot_ref, mix_ref):
    t0 = x[:, 0:8, :].reshape(LANE, LANE).T
    t1 = x[:, 8:16, :].reshape(LANE, LANE).T
    t2 = x[:, 16:24, :].reshape(LANE, LANE).T
    body = jnp.concatenate([t0, t1], axis=1)
    tail = jnp.concatenate([t2[:64], t2[64:]], axis=1)
    hits = []
    for i in range(NHIT):
        source, row = (body, 16 * i) if i < 8 else (tail, 16 * (i - 8))
        hits.append((source[row : row + 8], source[row + 8 : row + 16]))
    wide = 2 * LANE
    road = hits[0][1][7:8]
    each = lax.broadcasted_iota(jnp.int32, (ROADS, wide), 0).astype(F32)
    hot = jnp.where(each == road, 1.0, 0.0)
    start = jnp.sum(hot * off, axis=0, keepdims=True)
    rows = (lax.broadcasted_iota(jnp.int32, (ROADS * NPAR, wide), 0) >> 3).astype(F32)
    hot_ref[...] = jnp.where(rows == road, 1.0, 0.0).astype(BF16)
    slots = [jnp.broadcast_to(hits[i][1][6:7] - start, (8, wide)) for i in range(NHIT)]
    sums = []
    for s in range(ROAD):
        g = jnp.zeros((8, wide), F32)
        a = jnp.zeros((8, wide), F32)
        for i in range(NHIT):
            same = slots[i] == float(s)
            g = jnp.where(same, hits[i][0], g)
            a = jnp.where(same, hits[i][1], a)
        g_ref[8 * s : 8 * s + 8, :] = g
        t_ref[8 * s : 8 * s + 8, :] = 2.0 * g - g.astype(BF16).astype(F32)
        x_ref[0, 8 * s : 8 * s + 8, :] = a[:, :LANE]
        x_ref[1, 8 * s : 8 * s + 8, :] = a[:, LANE:]
        sums.append(g * a[5:6])
    v_hi, v_lo = split(jnp.concatenate(sums, axis=0))
    hot16 = hot.astype(BF16)
    road_rhs[...] += dot_t(hot16, v_hi) + dot_t(hot16, v_lo)
    lines = [
        jnp.concatenate(
            [x_ref[c, pl.ds(a, ROAD, stride=8), :] for c in range(2)], axis=1
        )
        for a in range(NLOC)
    ]

    ident = lax.broadcasted_iota(jnp.int32, (ROAD, wide), 0)
    for s in range(ROAD):
        mix = jnp.where(ident == s, 1.0, 0.0)
        for a in range(NLOC):
            mix = mix - lines[a][s : s + 1] * lines[a]
        mix_ref[ROAD * s : ROAD * s + ROAD, :] = mix

    for s in range(ROAD):
        at = slice(8 * s, 8 * s + 8)
        z = jnp.concatenate(
            [
                t_ref[8 * u : 8 * u + 8, :] * mix_ref[ROAD * s + u : ROAD * s + u + 1, :]
                for u in range(ROAD)
            ],
            axis=0,
        )
        z_both = jnp.concatenate(split(z), axis=0)
        g_s = g_ref[at, :]
        g_hi = jnp.concatenate([g_s, g_s], axis=0).astype(BF16)
        hot = hot_ref[...].reshape(ROADS // 2, 16, wide)
        left = (hot * g_hi[None]).reshape(ROADS * NPAR, wide)
        out = dot_t(left, z_both)
        blocks[:, at, :] += (out[:, :LANE] + out[:, LANE:]).reshape(ROADS, NPAR, LANE)


def symmetric(blocks, r):
    block = blocks[r]
    blocks[r] = 0.5 * (block + block.T)


HALF = 64
LINES = 80
OWN = slice(8, 72)


def low_lanes(x):
    return jnp.where(lax.broadcasted_iota(jnp.int32, x.shape, 1) < HALF, x, 0.0)


def spread(pieces, off, field):
    wide = jnp.concatenate([pieces, jnp.zeros_like(pieces)], axis=1)
    moved = jnp.where(off == 0.0, wide, 0.0)
    for d in range(1, NPAR):
        moved = jnp.where(off == float(d), pltpu.roll(wide, 8 * d, 1), moved)
    head, rest = moved[:, :LANE], moved[:, LANE:]
    field[80:88, :] = jnp.zeros((8, LANE), F32)
    field[0:80, :] = low_lanes(head)
    field[1:81, :] += low_lanes(pltpu.roll(head, HALF, 1))
    field[2:82, :] += low_lanes(rest)


def gather(field, off):
    head = field[0:80, :] + pltpu.roll(field[1:81, :], HALF, 1)
    wide = jnp.concatenate([head, field[2:82, :]], axis=1)
    piece = jnp.where(off == 0.0, wide, 0.0)
    for d in range(1, NPAR):
        piece = jnp.where(off == float(d), pltpu.roll(wide, 2 * LANE - 8 * d, 1), piece)
    return piece[:, :LANE]


def total(x):
    return jnp.sum(jnp.sum(x, axis=0, keepdims=True), axis=1, keepdims=True)


def to_rows(x, flat):
    for c in range(TRACKS // LANE):
        block = jnp.concatenate([x[:, c * LANE : (c + 1) * LANE], jnp.zeros((LANE - NPAR, LANE), F32)], axis=0)
        flat[c * LANE : (c + 1) * LANE, :] = block.T
    rows = flat[pl.ds(0, HALF, stride=8), :]
    for m in range(1, NPAR):
        rows = rows + pltpu.roll(flat[pl.ds(m, HALF, stride=8), :], 8 * m, 1)
    return rows


def from_rows(rows, flat):
    flat[pl.ds(0, HALF, stride=8), :] = rows
    for m in range(1, NPAR):
        flat[pl.ds(m, HALF, stride=8), :] = pltpu.roll(rows, LANE - 8 * m, 1)
    return jnp.concatenate(
        [flat[c * LANE : (c + 1) * LANE, :].T[:NPAR] for c in range(TRACKS // LANE)], axis=1
    )


def position():
    return lax.axis_index("trk"), lax.axis_index("mod")


def place_of(d):
    return (d // 8, lax.rem(d, 8))


def kernel_all(ld, gd, me_ref, hw, hm, hc, tr, rs, pw, blocks, rhs_out, cor_out,
               send, recv, lay, road_rhs, g_ref, t_ref, x_ref, hot_ref, mix_ref,
               part, vec, mapped, flat, info, info_prev, info_next, from_prev, from_next, blocks_prev, blocks_next,
               line, lines,
               send_sem, recv_sem, rim_sem, line_sem):
    trk, mod = position()
    me = trk * 8 + mod
    barrier = pltpu.get_barrier_semaphore()

    z, y, x, core = trk // 4, lax.rem(trk, 4), mod // 2, lax.rem(mod, 2)
    zs = [lax.rem(z + d, 4) * 4 for d in range(4)]
    ys = [lax.rem(y + d, 4) for d in range(4)]
    xs = [lax.rem(x + d, 4) * 2 for d in range(4)]
    cores = [core, 1 - core]
    trks = [zs[j // 4] + ys[j % 4] for j in range(GROUP)]
    mods = [xs[m // 2] + cores[m % 2] for m in range(8)]
    others = [(trks[j], mods[m]) for m in range(8) for j in range(GROUP) if j or m]
    for other in others:
        pl.semaphore_signal(barrier, inc=1, device_id=other, device_id_type=MESH)
    own = pltpu.make_async_copy(send.at[0], recv.at[0], recv_sem.at[0])

    def ready(step):
        if step == 0:
            pl.semaphore_wait(barrier, DEV - 1)
            own.start()
        for n in range(max(1, step * PLACED), (step + 1) * PLACED):
            c, j = n // GROUP, n % GROUP
            pltpu.make_async_remote_copy(
                send.at[n], recv.at[n], send_sem, recv_sem.at[c],
                device_id=(trks[j], mods[(c + j) % 8]), device_id_type=MESH,
            ).start()

    fit_and_place(ld, gd, me_ref, hw, hm, hc, tr, send, lay, trk, mod, ready)

    start = lax.rem(rs[...], NPAR).astype(F32)
    diagonal = lax.broadcasted_iota(jnp.int32, (ROADS, ROADS), 0) == lax.broadcasted_iota(
        jnp.int32, (ROADS, ROADS), 1
    )
    off = jnp.sum(jnp.where(diagonal, start, 0.0), axis=1, keepdims=True)
    nxt = place_of(lax.rem(me + 1, DEV))
    prv = place_of(lax.rem(me + DEV - 1, DEV))

    def to_next(source, target, n):
        return pltpu.make_async_remote_copy(
            source, target, rim_sem.at[n, 0], rim_sem.at[n, 1], device_id=nxt, device_id_type=MESH
        )

    def to_prev(source, target, n):
        return pltpu.make_async_remote_copy(
            source, target, rim_sem.at[n, 2], rim_sem.at[n, 3], device_id=prv, device_id_type=MESH
        )

    lanes = lax.broadcasted_iota(jnp.int32, (ROADS, LANE), 1)
    info[...] = jnp.where(lanes == HALF, off, to_rows(pw[...], flat))
    info_moves = (
        to_next(info.at[56:64], info_prev, 0),
        to_prev(info.at[0:8], info_next, 0),
    )
    for move in info_moves:
        move.start()
    mapped[...] = jnp.zeros_like(mapped)
    blocks[...] = jnp.zeros_like(blocks)
    road_rhs[...] = jnp.zeros_like(road_rhs)

    def take_group(c, carry):
        at = pl.ds(pl.multiple_of(c * GROUP, GROUP), GROUP)
        pltpu.make_async_copy(recv.at[at], recv.at[at], recv_sem.at[c]).wait()
        assemble(recv[at], off, blocks, road_rhs, g_ref, t_ref, x_ref, hot_ref, mix_ref)
        return carry

    lax.fori_loop(0, DEV // GROUP, take_group, 0)

    for move in info_moves:
        move.wait()
    edge = jnp.concatenate([info_prev[...], info[...], info_next[...]], axis=0)
    prior = low_lanes(edge)
    offs = edge[:, HALF : HALF + 1]

    mapped[OWN, :] = road_rhs[...]
    spread(mapped[...], offs, part)
    rim_moves = (to_next(part.at[64:80], from_prev, 1), to_prev(part.at[8:16], from_next, 1))
    for move in rim_moves:
        move.start()
    for r in (60, 61, 62, 63, 0, 1, 2, 3):
        symmetric(blocks, r)
    block_moves = (to_next(blocks.at[60:64], blocks_prev, 2), to_prev(blocks.at[0:2], blocks_next, 2))
    for move in block_moves:
        move.start()

    def symmetric_four(k, carry):
        for r in range(4):
            symmetric(blocks, 4 * k + r)
        return carry

    lax.fori_loop(1, 15, symmetric_four, 0)
    for move in rim_moves:
        move.wait()
    vec[0, 0:8, :] = from_prev[0:8, :]
    vec[0, 8:16, :] = part[8:16, :] + from_prev[8:16, :]
    vec[0, 16:72, :] = part[16:72, :]
    vec[0, 72:80, :] = part[72:80, :] + from_next[...]
    vec[0, 80:88, :] = jnp.zeros((8, LANE), F32)

    def apply(source, target, between):
        piece = gather(source, offs)
        flipped = jnp.concatenate([piece, jnp.zeros((LANE - LINES, LANE), F32)], axis=0).T

        def one(block, e):
            mapped[e : e + 1, :] = jnp.sum(block * flipped[:, e : e + 1], axis=0, keepdims=True)

        for r in range(ROADS):
            one(blocks[r], r + 8)
        between()
        for r in range(4):
            one(blocks_prev[r], r + 4)
        for r in range(2):
            one(blocks_next[r], r + 72)
        spread(mapped[...], offs, target)
        target[0:80, :] += prior * source[0:80, :]

    def take_blocks():
        rhs_out[...] = from_rows(vec[0, OWN, :], flat)
        for move in block_moves:
            move.wait()

    apply(vec.at[0], vec.at[1], take_blocks)
    apply(vec.at[1], vec.at[2], lambda: None)
    b, w, u = vec[0, OWN, :], vec[1, OWN, :], vec[2, OWN, :]

    def inverse(value):
        return jnp.where(value > 0.0, 1.0 / jnp.where(value > 0.0, value, 1.0), 0.0)

    bb, bw, bu = total(b * b), total(b * w), total(b * u)
    inv_bb = inverse(bb)
    w1 = w - (bw * inv_bb) * b
    u1 = u - (bu * inv_bb) * b
    ww, wu = total(w1 * w1), total(w1 * u1)
    u2 = u1 - (wu * inverse(ww)) * w1
    uu = total(u2 * u2)
    r11, r22 = jnp.sqrt(bb), jnp.sqrt(ww)
    lane = lax.broadcasted_iota(jnp.int32, (1, LANE), 1)
    row = jnp.zeros((1, LANE), F32)
    for n, value in enumerate((r11, bw * inverse(r11), bu * inverse(r11), r22, wu * inverse(r22), jnp.sqrt(uu))):
        row = jnp.where(lane == n, value, row)
    line[...] = row
    lines[me] = row
    for other in others:
        pltpu.make_async_remote_copy(
            line, lines.at[me], line_sem.at[0], line_sem.at[1], device_id=other, device_id_type=MESH
        ).start()
    w8 = from_rows(w, flat)
    whole = pltpu.make_async_remote_copy(
        lines.at[pl.ds(0, DEV - 1)], lines.at[pl.ds(0, DEV - 1)], line_sem.at[0], line_sem.at[1],
        device_id=nxt, device_id_type=MESH,
    )
    whole.wait_recv()
    for d in range(DEV):
        flat[d : d + 1, :] = lines[d]
    every = flat[0:DEV, :].T

    def add(x):
        return jnp.sum(x, axis=1, keepdims=True)

    b0, w0, u0, w1, u1, u2 = (every[n : n + 1, :] for n in range(6))
    square = add(b0 * b0) + EPS
    alpha_one = add(b0 * w0) / square
    beta_one = jnp.sqrt(square)
    inv_one = 1.0 / beta_one
    x0, x1 = (w0 - alpha_one * b0) * inv_one, w1 * inv_one
    beta_two = jnp.sqrt(add(x0 * x0 + x1 * x1) + EPS)
    inv_two = 1.0 / beta_two
    x0, x1 = x0 * inv_two, x1 * inv_two
    both_inv = inv_one * inv_two
    y0 = (u0 - alpha_one * w0) * both_inv - beta_two * inv_one * b0
    y1 = (u1 - alpha_one * w1) * both_inv
    y2 = u2 * both_inv
    alpha_two = add(x0 * y0 + x1 * y1)
    y0, y1 = y0 - alpha_two * x0, y1 - alpha_two * x1
    beta_three = jnp.sqrt(add(y0 * y0 + y1 * y1 + y2 * y2) + EPS)
    first = alpha_one * alpha_one + beta_two * beta_two
    cross = beta_two * (alpha_one + alpha_two)
    second = beta_two * beta_two + alpha_two * alpha_two + beta_three * beta_three
    determinant = first * second - cross * cross
    coef_one = beta_one * (second * alpha_one - cross * beta_two) / determinant
    coef_two = beta_one * (first * beta_two - cross * alpha_one) / determinant
    v1 = rhs_out[...] * inv_one
    v2 = (w8 * inv_one - alpha_one * v1) * inv_two
    cor_out[...] = coef_one * v1 + coef_two * v2
    whole.wait_send()
    sent = pltpu.make_async_remote_copy(
        send.at[pl.ds(0, DEV - 1)], recv.at[pl.ds(0, DEV - 1)], send_sem, recv_sem.at[0],
        device_id=nxt, device_id_type=MESH,
    )
    sent.wait_send()


VM = pl.BlockSpec(memory_space=pltpu.VMEM)


def on_device(ld, gd, me, hw, hm, hc, tr, rs, pw):
    def vmem(*shape, dtype=F32):
        return pltpu.VMEM(shape, dtype)

    blocks, rhs, cor = pl.pallas_call(
        kernel_all,
        out_shape=(
            jax.ShapeDtypeStruct((ROADS, LANE, LANE), F32),
            jax.ShapeDtypeStruct((NPAR, TRACKS), F32),
            jax.ShapeDtypeStruct((NPAR, TRACKS), F32),
        ),
        in_specs=[VM] * 9,
        out_specs=(VM, VM, VM),
        scratch_shapes=[
            vmem(DEV, 24, LANE),
            vmem(DEV, 24, LANE),
            vmem(4, 192, LANE),
            vmem(ROADS, LANE),
            vmem(LANE, 2 * LANE),
            vmem(LANE, 2 * LANE),
            vmem(2, LANE, LANE),
            vmem(ROADS * NPAR, 2 * LANE, dtype=BF16),
            vmem(ROAD * ROAD, 2 * LANE),
            vmem(88, LANE),
            vmem(3, 88, LANE),
            vmem(LINES, LANE),
            vmem(TRACKS, LANE),
            vmem(ROADS, LANE),
            vmem(8, LANE),
            vmem(8, LANE),
            vmem(16, LANE),
            vmem(8, LANE),
            vmem(4, LANE, LANE),
            vmem(2, LANE, LANE),
            vmem(1, LANE),
            vmem(DEV, 1, LANE),
            pltpu.SemaphoreType.DMA,
            pltpu.SemaphoreType.DMA((DEV // GROUP,)),
            pltpu.SemaphoreType.DMA((3, 4)),
            pltpu.SemaphoreType.DMA((2,)),
        ],
        compiler_params=pltpu.CompilerParams(collective_id=0, has_side_effects=True, vmem_limit_bytes=32 * 1024 * 1024),
        name="alignment",
    )(*(pltpu.with_memory_space_constraint(array, pltpu.HBM) for array in (
        ld,
        jnp.transpose(gd, (1, 0, 2)),
        me,
        hw,
        hm,
        hc.reshape(1, TRACKS),
        tr.reshape(1, TRACKS),
        rs.reshape(1, ROADS),
        pw.T,
    )))
    return blocks, rhs.T, cor.T


def solution(mesh):
    both = ("trk", "mod")
    in_specs = (
        P(None, None, both),
        P(None, None, both),
        P(None, both),
        P(None, both),
        P(None, both),
        P(both),
        P(both),
        P(both),
        P(both, None),
    )
    out_specs = (P(both, None, None), P(both, None), P(both, None))
    return jax.shard_map(on_device, mesh=mesh, in_specs=in_specs, out_specs=out_specs, check_vma=False)
```

```python
import functools

import jax
import jax.numpy as jnp
from jax import lax
from jax.experimental import pallas as pl
from jax.experimental.pallas import tpu as pltpu
from jax.sharding import PartitionSpec as P

F32 = jnp.float32
BF16 = jnp.bfloat16
NPAR = 8
NLOC = 5
NHIT = 12
ROAD = 16
CAP = 16
LANE = 128
NMOD = 65536
ROADS = 64
TRACKS = 512
DEV = 128
GROUP = 16
PLACED = 32
EPS = 1e-6
MESH = pl.DeviceIdType.MESH
CONTRACT_LANES = (((1,), (1,)), ((), ()))


def dot_t(a, b):
    return lax.dot_general(a, b, CONTRACT_LANES, preferred_element_type=F32)


def split(x):
    hi = x.astype(BF16)
    return hi, (x - hi.astype(F32)).astype(BF16)


def fit_and_place(ld, gd, me, hw, hm, hc, tr, send, lay, trk, mod, ready):
    position = lax.broadcasted_iota(jnp.int32, (NHIT, TRACKS), 0)
    live = position < hc[...]
    root = jnp.where(live, jnp.sqrt(hw[...]), 0.0)
    scaled = [ld[a] * root for a in range(NLOC)]
    factor = {}
    for i in range(NLOC):
        for j in range(i + 1):
            running = jnp.sum(scaled[i] * scaled[j], axis=0, keepdims=True)
            if i == j:
                running = running + 1.0
            for k in range(j):
                running = running - factor[i, k] * factor[j, k]
            factor[i, j] = jnp.sqrt(running) if i == j else running / factor[j, j]
    proj = []
    for i in range(NLOC):
        running = scaled[i]
        for j in range(i):
            running = running - factor[i, j] * proj[j]
        proj.append(running / factor[i, i])
    resid = me[...] * root
    solved = resid
    for a in range(NLOC):
        solved = solved - proj[a] * jnp.sum(proj[a] * resid, axis=0, keepdims=True)
    road = tr[...]
    rel = lax.rem(hm[...] - NPAR * road + NMOD, NMOD).astype(F32)
    local_road = jnp.broadcast_to((road & (ROADS - 1)).astype(F32), (NHIT, TRACKS))
    words = proj + [solved, rel, local_road]
    for c in range(TRACKS // LANE):
        at = slice(c * LANE, (c + 1) * LANE)
        for i in range(NHIT):
            lay[c, 16 * i : 16 * i + 8, :] = gd[i, :, at] * root[i : i + 1, at]
        for w, value in enumerate(words):
            lay[c, pl.ds(8 + w, 8, stride=16), :] = value[:8, at]
            lay[c, pl.ds(LANE + 8 + w, 4, stride=16), :] = value[8:, at]
    whole = jnp.concatenate([lay[c] for c in range(TRACKS // LANE)], axis=1)
    tail = whole[LANE:]
    none = jnp.zeros_like(tail)

    def both(value):
        return jnp.concatenate(split(value), axis=0)

    first_w = both(whole[:LANE])
    left_w = both(jnp.concatenate([tail, none], axis=0))
    right_w = both(jnp.concatenate([none, tail], axis=0))

    owner = road >> 6
    z, y, x, core = trk // 4, lax.rem(trk, 4), mod // 2, lax.rem(mod, 2)
    j = (((owner >> 5) - z) & 3) * 4 + (((owner >> 3) - y) & 3)
    m = (((owner >> 1) - x) & 3) * 2 + ((owner - core) & 1)
    chunk = ((m - j) & 7) * GROUP + j
    member = jnp.where(lax.broadcasted_iota(jnp.int32, (DEV, TRACKS), 0) == chunk, 1.0, 0.0)
    earlier = lax.broadcasted_iota(jnp.int32, (TRACKS, TRACKS), 0) <= lax.broadcasted_iota(
        jnp.int32, (TRACKS, TRACKS), 1
    )
    running = jnp.dot(
        member.astype(BF16), jnp.where(earlier, 1.0, 0.0).astype(BF16), preferred_element_type=F32
    )
    rank = jnp.sum(member * running, axis=0, keepdims=True) - 1.0
    slot = chunk * CAP + rank.astype(jnp.int32)

    for step in range(DEV // PLACED):
        row = lax.broadcasted_iota(jnp.int32, (PLACED * CAP, TRACKS), 0) + step * (PLACED * CAP)
        chosen = jnp.where(row == slot, 1.0, 0.0)
        halves = chosen.reshape(PLACED, 2, 8, TRACKS)
        low = halves[:, 0].reshape(PLACED * 8, TRACKS).astype(BF16)
        high = halves[:, 1].reshape(PLACED * 8, TRACKS).astype(BF16)
        first = dot_t(chosen.astype(BF16), first_w)
        last = dot_t(low, left_w) + dot_t(high, right_w)
        at = slice(step * PLACED, (step + 1) * PLACED)
        send[at, 0:16, :] = (first[:, :LANE] + first[:, LANE:]).reshape(PLACED, CAP, LANE)
        send[at, 16:24, :] = (last[:, :LANE] + last[:, LANE:]).reshape(PLACED, 8, LANE)
        ready(step)


def assemble(x, off, blocks, road_rhs, g_ref, t_ref, x_ref, hot_ref, mix_ref):
    t0 = x[:, 0:8, :].reshape(LANE, LANE).T
    t1 = x[:, 8:16, :].reshape(LANE, LANE).T
    t2 = x[:, 16:24, :].reshape(LANE, LANE).T
    body = jnp.concatenate([t0, t1], axis=1)
    tail = jnp.concatenate([t2[:64], t2[64:]], axis=1)
    hits = []
    for i in range(NHIT):
        source, row = (body, 16 * i) if i < 8 else (tail, 16 * (i - 8))
        hits.append((source[row : row + 8], source[row + 8 : row + 16]))
    wide = 2 * LANE
    road = hits[0][1][7:8]
    each = lax.broadcasted_iota(jnp.int32, (ROADS, wide), 0).astype(F32)
    hot = jnp.where(each == road, 1.0, 0.0)
    start = jnp.sum(hot * off, axis=0, keepdims=True)
    rows = (lax.broadcasted_iota(jnp.int32, (ROADS * NPAR, wide), 0) >> 3).astype(F32)
    hot_ref[...] = jnp.where(rows == road, 1.0, 0.0).astype(BF16)
    slots = [jnp.broadcast_to(hits[i][1][6:7] - start, (8, wide)) for i in range(NHIT)]
    sums = []
    for s in range(ROAD):
        g = jnp.zeros((8, wide), F32)
        a = jnp.zeros((8, wide), F32)
        for i in range(NHIT):
            same = slots[i] == float(s)
            g = jnp.where(same, hits[i][0], g)
            a = jnp.where(same, hits[i][1], a)
        g_ref[8 * s : 8 * s + 8, :] = g
        t_ref[8 * s : 8 * s + 8, :] = 2.0 * g - g.astype(BF16).astype(F32)
        x_ref[0, 8 * s : 8 * s + 8, :] = a[:, :LANE]
        x_ref[1, 8 * s : 8 * s + 8, :] = a[:, LANE:]
        sums.append(g * a[5:6])
    v_hi, v_lo = split(jnp.concatenate(sums, axis=0))
    hot16 = hot.astype(BF16)
    road_rhs[...] += dot_t(hot16, v_hi) + dot_t(hot16, v_lo)
    lines = [
        jnp.concatenate(
            [x_ref[c, pl.ds(a, ROAD, stride=8), :] for c in range(2)], axis=1
        )
        for a in range(NLOC)
    ]

    ident = lax.broadcasted_iota(jnp.int32, (ROAD, wide), 0)
    for s in range(ROAD):
        mix = jnp.where(ident == s, 1.0, 0.0)
        for a in range(NLOC):
            mix = mix - lines[a][s : s + 1] * lines[a]
        mix_ref[ROAD * s : ROAD * s + ROAD, :] = mix

    for s in range(ROAD):
        at = slice(8 * s, 8 * s + 8)
        z = jnp.concatenate(
            [
                t_ref[8 * u : 8 * u + 8, :] * mix_ref[ROAD * s + u : ROAD * s + u + 1, :]
                for u in range(ROAD)
            ],
            axis=0,
        )
        z_both = jnp.concatenate(split(z), axis=0)
        g_s = g_ref[at, :]
        g_hi = jnp.concatenate([g_s, g_s], axis=0).astype(BF16)
        hot = hot_ref[...].reshape(ROADS // 2, 16, wide)
        left = (hot * g_hi[None]).reshape(ROADS * NPAR, wide)
        out = dot_t(left, z_both)
        blocks[:, at, :] += (out[:, :LANE] + out[:, LANE:]).reshape(ROADS, NPAR, LANE)


def symmetric(blocks, r):
    block = blocks[r]
    blocks[r] = 0.5 * (block + block.T)


HALF = 64
LINES = 80
OWN = slice(8, 72)


def low_lanes(x):
    return jnp.where(lax.broadcasted_iota(jnp.int32, x.shape, 1) < HALF, x, 0.0)


def spread(pieces, off, field):
    wide = jnp.concatenate([pieces, jnp.zeros_like(pieces)], axis=1)
    moved = jnp.where(off == 0.0, wide, 0.0)
    for d in range(1, NPAR):
        moved = jnp.where(off == float(d), pltpu.roll(wide, 8 * d, 1), moved)
    head, rest = moved[:, :LANE], moved[:, LANE:]
    field[80:88, :] = jnp.zeros((8, LANE), F32)
    field[0:80, :] = low_lanes(head)
    field[1:81, :] += low_lanes(pltpu.roll(head, HALF, 1))
    field[2:82, :] += low_lanes(rest)


def gather(field, off):
    head = field[0:80, :] + pltpu.roll(field[1:81, :], HALF, 1)
    wide = jnp.concatenate([head, field[2:82, :]], axis=1)
    piece = jnp.where(off == 0.0, wide, 0.0)
    for d in range(1, NPAR):
        piece = jnp.where(off == float(d), pltpu.roll(wide, 2 * LANE - 8 * d, 1), piece)
    return piece[:, :LANE]


def total(x):
    return jnp.sum(jnp.sum(x, axis=0, keepdims=True), axis=1, keepdims=True)


def to_rows(x, flat):
    for c in range(TRACKS // LANE):
        block = jnp.concatenate([x[:, c * LANE : (c + 1) * LANE], jnp.zeros((LANE - NPAR, LANE), F32)], axis=0)
        flat[c * LANE : (c + 1) * LANE, :] = block.T
    rows = flat[pl.ds(0, HALF, stride=8), :]
    for m in range(1, NPAR):
        rows = rows + pltpu.roll(flat[pl.ds(m, HALF, stride=8), :], 8 * m, 1)
    return rows


def from_rows(rows, flat):
    flat[pl.ds(0, HALF, stride=8), :] = rows
    for m in range(1, NPAR):
        flat[pl.ds(m, HALF, stride=8), :] = pltpu.roll(rows, LANE - 8 * m, 1)
    return jnp.concatenate(
        [flat[c * LANE : (c + 1) * LANE, :].T[:NPAR] for c in range(TRACKS // LANE)], axis=1
    )


def position():
    return lax.axis_index("trk"), lax.axis_index("mod")


def place_of(d):
    return (d // 8, lax.rem(d, 8))


def kernel_all(ld, gd, me_ref, hw, hm, hc, tr, rs, pw, blocks, pair,
               send, recv, lay, road_rhs, g_ref, t_ref, x_ref, hot_ref, mix_ref,
               part, vec, mapped, flat, info, info_prev, info_next, from_prev, from_next, blocks_prev, blocks_next,
               line, lines,
               send_sem, recv_sem, rim_sem, line_sem):
    trk, mod = position()
    me = trk * 8 + mod
    barrier = pltpu.get_barrier_semaphore()

    z, y, x, core = trk // 4, lax.rem(trk, 4), mod // 2, lax.rem(mod, 2)
    zs = [lax.rem(z + d, 4) * 4 for d in range(4)]
    ys = [lax.rem(y + d, 4) for d in range(4)]
    xs = [lax.rem(x + d, 4) * 2 for d in range(4)]
    cores = [core, 1 - core]
    trks = [zs[j // 4] + ys[j % 4] for j in range(GROUP)]
    mods = [xs[m // 2] + cores[m % 2] for m in range(8)]
    step_cost = (0, 1, 2, 1)
    far_first = sorted(
        (-step_cost[j // 4] - step_cost[j % 4] - step_cost[m // 2], j, m) for m in range(8) for j in range(GROUP) if j or m
    )
    others = [(trks[j], mods[m]) for _, j, m in far_first]
    for other in others:
        pl.semaphore_signal(barrier, inc=1, device_id=other, device_id_type=MESH)
    own = pltpu.make_async_copy(send.at[0], recv.at[0], recv_sem.at[0])

    def ready(step):
        if step == 0:
            pl.semaphore_wait(barrier, DEV - 1)
            own.start()
        for n in range(max(1, step * PLACED), (step + 1) * PLACED):
            c, j = n // GROUP, n % GROUP
            pltpu.make_async_remote_copy(
                send.at[n], recv.at[n], send_sem, recv_sem.at[c],
                device_id=(trks[j], mods[(c + j) % 8]), device_id_type=MESH,
            ).start()

    fit_and_place(ld, gd, me_ref, hw, hm, hc, tr, send, lay, trk, mod, ready)

    start = lax.rem(rs[...], NPAR).astype(F32)
    diagonal = lax.broadcasted_iota(jnp.int32, (ROADS, ROADS), 0) == lax.broadcasted_iota(
        jnp.int32, (ROADS, ROADS), 1
    )
    off = jnp.sum(jnp.where(diagonal, start, 0.0), axis=1, keepdims=True)
    nxt = place_of(lax.rem(me + 1, DEV))
    prv = place_of(lax.rem(me + DEV - 1, DEV))

    def to_next(source, target, n):
        return pltpu.make_async_remote_copy(
            source, target, rim_sem.at[n, 0], rim_sem.at[n, 1], device_id=nxt, device_id_type=MESH
        )

    def to_prev(source, target, n):
        return pltpu.make_async_remote_copy(
            source, target, rim_sem.at[n, 2], rim_sem.at[n, 3], device_id=prv, device_id_type=MESH
        )

    lanes = lax.broadcasted_iota(jnp.int32, (ROADS, LANE), 1)
    info[...] = jnp.where(lanes == HALF, off, to_rows(pw[...], flat))
    info_moves = (
        to_next(info.at[56:64], info_prev, 0),
        to_prev(info.at[0:8], info_next, 0),
    )
    for move in info_moves:
        move.start()
    mapped[...] = jnp.zeros_like(mapped)
    blocks[...] = jnp.zeros_like(blocks)
    road_rhs[...] = jnp.zeros_like(road_rhs)

    def take_group(c, carry):
        at = pl.ds(pl.multiple_of(c * GROUP, GROUP), GROUP)
        pltpu.make_async_copy(recv.at[at], recv.at[at], recv_sem.at[c]).wait()
        assemble(recv[at], off, blocks, road_rhs, g_ref, t_ref, x_ref, hot_ref, mix_ref)
        return carry

    lax.fori_loop(0, DEV // GROUP, take_group, 0)

    for move in info_moves:
        move.wait()
    edge = jnp.concatenate([info_prev[...], info[...], info_next[...]], axis=0)
    prior = low_lanes(edge)
    offs = edge[:, HALF : HALF + 1]

    mapped[OWN, :] = road_rhs[...]
    spread(mapped[...], offs, part)
    rim_moves = (to_next(part.at[64:80], from_prev, 1), to_prev(part.at[8:16], from_next, 1))
    for move in rim_moves:
        move.start()
    for r in (60, 61, 62, 63, 0, 1, 2, 3):
        symmetric(blocks, r)
    block_moves = (to_next(blocks.at[60:64], blocks_prev, 2), to_prev(blocks.at[0:2], blocks_next, 2))
    for move in block_moves:
        move.start()

    def symmetric_four(k, carry):
        for r in range(4):
            symmetric(blocks, 4 * k + r)
        return carry

    lax.fori_loop(1, 15, symmetric_four, 0)
    for move in rim_moves:
        move.wait()
    vec[0, 0:8, :] = from_prev[0:8, :]
    vec[0, 8:16, :] = part[8:16, :] + from_prev[8:16, :]
    vec[0, 16:72, :] = part[16:72, :]
    vec[0, 72:80, :] = part[72:80, :] + from_next[...]
    vec[0, 80:88, :] = jnp.zeros((8, LANE), F32)

    def apply(source, target, between):
        piece = gather(source, offs)
        flipped = jnp.concatenate([piece, jnp.zeros((LANE - LINES, LANE), F32)], axis=0).T

        def one(block, e):
            mapped[e : e + 1, :] = jnp.sum(block * flipped[:, e : e + 1], axis=0, keepdims=True)

        for r in range(ROADS):
            one(blocks[r], r + 8)
        between()
        for r in range(4):
            one(blocks_prev[r], r + 4)
        for r in range(2):
            one(blocks_next[r], r + 72)
        spread(mapped[...], offs, target)
        target[0:80, :] += prior * source[0:80, :]

    def take_blocks():
        pair[0:8, :] = from_rows(vec[0, OWN, :], flat)
        for move in block_moves:
            move.wait()

    apply(vec.at[0], vec.at[1], take_blocks)
    apply(vec.at[1], vec.at[2], lambda: None)
    b, w, u = vec[0, OWN, :], vec[1, OWN, :], vec[2, OWN, :]

    def inverse(value):
        return jnp.where(value > 0.0, 1.0 / jnp.where(value > 0.0, value, 1.0), 0.0)

    bb, bw, bu = total(b * b), total(b * w), total(b * u)
    inv_bb = inverse(bb)
    w1 = w - (bw * inv_bb) * b
    u1 = u - (bu * inv_bb) * b
    ww, wu = total(w1 * w1), total(w1 * u1)
    u2 = u1 - (wu * inverse(ww)) * w1
    uu = total(u2 * u2)
    r11, r22 = jnp.sqrt(bb), jnp.sqrt(ww)
    lane = lax.broadcasted_iota(jnp.int32, (1, LANE), 1)
    row = jnp.zeros((1, LANE), F32)
    for n, value in enumerate((r11, bw * inverse(r11), bu * inverse(r11), r22, wu * inverse(r22), jnp.sqrt(uu))):
        row = jnp.where(lane == n, value, row)
    line[...] = row
    lines[me] = row
    for other in others:
        pltpu.make_async_remote_copy(
            line, lines.at[me], line_sem.at[0], line_sem.at[1], device_id=other, device_id_type=MESH
        ).start()
    w8 = from_rows(w, flat)
    whole = pltpu.make_async_remote_copy(
        lines.at[pl.ds(0, DEV - 1)], lines.at[pl.ds(0, DEV - 1)], line_sem.at[0], line_sem.at[1],
        device_id=nxt, device_id_type=MESH,
    )
    whole.wait_recv()
    for d in range(DEV):
        flat[d : d + 1, :] = lines[d]
    every = flat[0:DEV, :].T

    def add(x):
        return jnp.sum(x, axis=1, keepdims=True)

    b0, w0, u0, w1, u1, u2 = (every[n : n + 1, :] for n in range(6))
    square = add(b0 * b0) + EPS
    alpha_one = add(b0 * w0) / square
    beta_one = jnp.sqrt(square)
    inv_one = 1.0 / beta_one
    x0, x1 = (w0 - alpha_one * b0) * inv_one, w1 * inv_one
    beta_two = jnp.sqrt(add(x0 * x0 + x1 * x1) + EPS)
    inv_two = 1.0 / beta_two
    x0, x1 = x0 * inv_two, x1 * inv_two
    both_inv = inv_one * inv_two
    y0 = (u0 - alpha_one * w0) * both_inv - beta_two * inv_one * b0
    y1 = (u1 - alpha_one * w1) * both_inv
    y2 = u2 * both_inv
    alpha_two = add(x0 * y0 + x1 * y1)
    y0, y1 = y0 - alpha_two * x0, y1 - alpha_two * x1
    beta_three = jnp.sqrt(add(y0 * y0 + y1 * y1 + y2 * y2) + EPS)
    first = alpha_one * alpha_one + beta_two * beta_two
    cross = beta_two * (alpha_one + alpha_two)
    second = beta_two * beta_two + alpha_two * alpha_two + beta_three * beta_three
    determinant = first * second - cross * cross
    coef_one = beta_one * (second * alpha_one - cross * beta_two) / determinant
    coef_two = beta_one * (first * beta_two - cross * alpha_one) / determinant
    v1 = pair[0:8, :] * inv_one
    v2 = (w8 * inv_one - alpha_one * v1) * inv_two
    pair[8:16, :] = coef_one * v1 + coef_two * v2
    whole.wait_send()
    sent = pltpu.make_async_remote_copy(
        send.at[pl.ds(0, DEV - 1)], recv.at[pl.ds(0, DEV - 1)], send_sem, recv_sem.at[0],
        device_id=nxt, device_id_type=MESH,
    )
    sent.wait_send()


VM = pl.BlockSpec(memory_space=pltpu.VMEM)


def on_device(ld, gd, me, hw, hm, hc, tr, rs, pw):
    def vmem(*shape, dtype=F32):
        return pltpu.VMEM(shape, dtype)

    blocks, pair = pl.pallas_call(
        kernel_all,
        out_shape=(
            jax.ShapeDtypeStruct((ROADS, LANE, LANE), F32),
            jax.ShapeDtypeStruct((2 * NPAR, TRACKS), F32),
        ),
        in_specs=[VM] * 9,
        out_specs=(VM, VM),
        scratch_shapes=[
            vmem(DEV, 24, LANE),
            vmem(DEV, 24, LANE),
            vmem(4, 192, LANE),
            vmem(ROADS, LANE),
            vmem(LANE, 2 * LANE),
            vmem(LANE, 2 * LANE),
            vmem(2, LANE, LANE),
            vmem(ROADS * NPAR, 2 * LANE, dtype=BF16),
            vmem(ROAD * ROAD, 2 * LANE),
            vmem(88, LANE),
            vmem(3, 88, LANE),
            vmem(LINES, LANE),
            vmem(TRACKS, LANE),
            vmem(ROADS, LANE),
            vmem(8, LANE),
            vmem(8, LANE),
            vmem(16, LANE),
            vmem(8, LANE),
            vmem(4, LANE, LANE),
            vmem(2, LANE, LANE),
            vmem(1, LANE),
            vmem(DEV, 1, LANE),
            pltpu.SemaphoreType.DMA,
            pltpu.SemaphoreType.DMA((DEV // GROUP,)),
            pltpu.SemaphoreType.DMA((3, 4)),
            pltpu.SemaphoreType.DMA((2,)),
        ],
        compiler_params=pltpu.CompilerParams(collective_id=0, has_side_effects=True, vmem_limit_bytes=32 * 1024 * 1024),
        name="alignment",
    )(*(pltpu.with_memory_space_constraint(array, pltpu.HBM) for array in (
        ld,
        jnp.transpose(gd, (1, 0, 2)),
        me,
        hw,
        hm,
        hc.reshape(1, TRACKS),
        tr.reshape(1, TRACKS),
        rs.reshape(1, ROADS),
        pw.T,
    )))
    return blocks, pair[:NPAR].T, pair[NPAR:].T


def solution(mesh):
    both = ("trk", "mod")
    in_specs = (
        P(None, None, both),
        P(None, None, both),
        P(None, both),
        P(None, both),
        P(None, both),
        P(both),
        P(both),
        P(both),
        P(both, None),
    )
    out_specs = (P(both, None, None), P(both, None), P(both, None))
    return jax.shard_map(on_device, mesh=mesh, in_specs=in_specs, out_specs=out_specs, check_vma=False)
```
